32 devices in a mesh: groups: 2 (over y), vocab: 4 (over z), tokens: 2 (over x), section: 2 (over core).
Axes of the slice: x: 2, y: 2, z: 4, core: 2. Of those that a mesh axis runs over, the one named last changes fastest.
Arguments:
- teacher_hidden: bfloat16 [512, 16384], P(('groups', 'vocab', 'section'), 'tokens'), parts along dimension 0
- teacher_weight: bfloat16 [16384, 4096], P('tokens', ('vocab', 'section'))
- student_hidden: bfloat16 [512, 4096], P(('groups', 'tokens')), parts along dimension 0
- student_gain: float32 [4096], replicated, may hold values from 0.5 to 1.5
- student_weight: bfloat16 [4096, 4096], P('tokens', ('vocab', 'section'))
- labels: int32 [512], P(('groups', 'tokens')), parts along dimension 0, may hold values from 0 to 4095
- alignment: int32 [512], P(('groups', 'tokens')), parts along dimension 0, may hold values from 0 to 255, as said below
- loss_mask: int32 [512], P('groups'), parts along dimension 0, may hold values from 0 to 1, as said below
Outputs:
- row_loss: float32 [512], P(('groups', 'tokens')), parts along dimension 0
- logit_grad: bfloat16 [512, 4096], P(('groups', 'tokens'), ('vocab', 'section')), parts along dimension 0
- hidden_grad: bfloat16 [512, 4096], P(('groups', 'tokens'), ('vocab', 'section')), parts along dimension 0
The draws below stay inside these ranges and needn't reach their ends.
There are 2 independent parts, one for each index of `groups`. The reference program is written for one: setup_inputs(seed, part) draws one part's arguments, and reference() takes and returns one part's arrays. A program takes and returns all parts, laid end to end along the dimension named above; an argument that names none is the same for every part. Nothing has to cross between parts.
Inputs may be any that keep to these rules, and one draw needn't show every extreme that they name: Within each aligned block of 128 frames the alignment never falls, names only tokens of the same block, and starts at the block's first token and ends at its last. `loss_mask`: the last frame always counts.
All inputs are finite; a program needn't handle non-finite values.
Results may differ from the reference program's by a relative error of at most 0.0061.
Values may be sent and summed in bfloat16 or wider, within the bound.
A program may use at most 64 MiB of HBM per device.

```python
import math
import jax
import jax.numpy as jnp
from jax import lax

DT = 16384
DS = 4096
TOK_DEV = 128
TOK = 256
V = 4096


def drawn_values(key, rows, width, factor):
    return jnp.clip(jax.random.normal(key, (rows, width), jnp.float32), -5.0, 5.0) * factor


def draw_teacher_hidden(key, part):
    own_key = jax.random.fold_in(key, 101)
    values = drawn_values(own_key, TOK, DT, 1.0)
    return values.astype(jnp.bfloat16)


def draw_student_hidden(key, part):
    own_key = jax.random.fold_in(key, 202)
    values = drawn_values(own_key, TOK, DS, 1.0)
    return values.astype(jnp.bfloat16)


def draw_teacher_weight(key, part):
    own_key = jax.random.fold_in(key, 303)
    values = drawn_values(own_key, DT, V, 3.0 / math.sqrt(DT))
    return values.astype(jnp.bfloat16)


def draw_student_weight(key, part):
    own_key = jax.random.fold_in(key, 404)
    values = drawn_values(own_key, DS, V, 3.0 / math.sqrt(DS))
    return values.astype(jnp.bfloat16)


def draw_alignment(key, part):
    blocks = TOK // TOK_DEV
    offsets = jnp.sort(jax.random.randint(key, (blocks, TOK_DEV), 0, TOK_DEV), axis=1)
    position = jnp.arange(TOK_DEV, dtype=jnp.int32)[None, :]
    offsets = jnp.where(position == 0, 0, jnp.where(position == TOK_DEV - 1, TOK_DEV - 1, offsets))
    starts = jnp.arange(blocks, dtype=jnp.int32)[:, None] * TOK_DEV
    return (starts + offsets).reshape(TOK).astype(jnp.int32)


def draw_loss_mask(key, part):
    values = jax.random.randint(key, (TOK,), 0, 3 * TOK - 3)
    limits = 3 * jnp.arange(TOK, dtype=jnp.int32)
    return (values < limits).astype(jnp.int32)


def touch_ends(entries, stream_key, low, top_value):
    shape = entries.shape
    index_at = [jax.random.randint(jax.random.fold_in(stream_key, axis), (), 0, shape[axis]) for axis in range(len(shape))]
    entries = entries.at[tuple(index_at)].set(low)
    longest = shape.index(max(shape))
    index_at[longest] = (index_at[longest] + 1) % shape[longest]
    return entries.at[tuple(index_at)].set(top_value)


def setup_inputs(seed: int = 0, part: int = 0) -> dict:
    arg_keys = jax.random.split(jax.random.key(seed), 9)
    part_keys = jax.random.split(jax.random.fold_in(arg_keys[8], part), 9)
    return {
        "teacher_hidden": draw_teacher_hidden(jax.random.fold_in(jax.random.fold_in(arg_keys[8], part), 71), part),
        "teacher_weight": draw_teacher_weight(jax.random.fold_in(arg_keys[8], 71), part),
        "student_hidden": draw_student_hidden(jax.random.fold_in(jax.random.fold_in(arg_keys[8], part), 71), part),
        "student_gain": jnp.clip(1.0 + 0.1 * jax.random.normal(arg_keys[3], (DS,), jnp.float32), 0.5, 1.5),
        "student_weight": draw_student_weight(jax.random.fold_in(arg_keys[8], 71), part),
        "labels": touch_ends(jax.random.randint(part_keys[5], (TOK,), 0, V), jax.random.fold_in(part_keys[5], 1), 0, V - 1).astype(jnp.int32),
        "alignment": draw_alignment(jax.random.fold_in(jax.random.fold_in(arg_keys[8], part), 71), part),
        "loss_mask": draw_loss_mask(jax.random.fold_in(jax.random.fold_in(arg_keys[8], part), 71), part),
    }


label_weight = 0.2
loss_scale = 16.0
epsilon = 1e-05

def reference(teacher_hidden, teacher_weight, student_hidden, student_gain, student_weight, labels, alignment, loss_mask):
    aligned = jnp.dot(teacher_hidden[alignment], teacher_weight, preferred_element_type=jnp.float32)
    hidden = student_hidden.astype(jnp.float32)
    inverse = lax.rsqrt(lax.optimization_barrier(jnp.mean(hidden * hidden, axis=1, keepdims=True)) + epsilon)
    normed = (hidden * inverse * student_gain).astype(jnp.bfloat16)
    student = jnp.dot(normed, student_weight, preferred_element_type=jnp.float32)
    lse_t = jax.nn.logsumexp(aligned, axis=1)
    lse_s = jax.nn.logsumexp(student, axis=1)
    teacher_prob = jnp.exp(aligned - lse_t[:, None])
    student_prob = jnp.exp(student - lse_s[:, None])
    diverge = lax.optimization_barrier(jnp.sum(teacher_prob * (aligned - student), axis=1)) - lse_t + lse_s
    onehot = labels[:, None] == jnp.arange(student.shape[1], dtype=jnp.int32)[None, :]
    label_logit = lax.optimization_barrier(jnp.sum(jnp.where(onehot, student, 0.0), axis=1))
    cross_term = lse_s - label_logit
    mask_float = loss_mask.astype(jnp.float32)
    mask_count = jnp.sum(mask_float)
    row_weight = mask_float * loss_mask.shape[0] / mask_count
    row_loss = row_weight * (diverge + label_weight * cross_term)
    onehot_float = onehot.astype(jnp.float32)
    logit_grad = (loss_scale * row_weight[:, None] * ((1.0 + label_weight) * student_prob - teacher_prob - label_weight * onehot_float)).astype(jnp.bfloat16)
    normed_grad = jnp.dot(logit_grad, student_weight.T, preferred_element_type=jnp.float32)
    scaled = normed_grad * student_gain
    inner_rows = lax.optimization_barrier(jnp.sum(scaled * hidden, axis=1, keepdims=True))
    hidden_grad = (inverse * scaled - hidden * inverse ** 3 * inner_rows / hidden.shape[1]).astype(jnp.bfloat16)
    return (row_loss, logit_grad, hidden_grad)
```

```python
import functools

import jax
import jax.numpy as jnp
from jax import lax
from jax.experimental import pallas as pl
from jax.experimental.pallas import tpu as pltpu
from jax.sharding import PartitionSpec as P

label_weight = 0.2
loss_scale = 16.0
epsilon = 1e-05
MESH = pl.DeviceIdType.MESH


def kernel(
    sizes, th, tw, sh_in, gain_in, sw, labels_in, align_in, mask_in,
    rl_hbm, out_hbm,
    sh, gain, labels, align, mask, rl_out, lg_out, hg_out,
    tbuf, twv, wbuf, normed, acc, tin, bl, stats, inner_in, sibout, sibin, part, rin, lin, inner_acc,
    tw_sem, own_sem, sw_sem, in_sem, out_sem,
    left_send, right_send, sib_send, z_recv, s_recv,
    x_send, x_recv, y_send, y_recv,
    acc_send, acc_recv,
    stat_send, stat_recv, inner_send, inner_recv,
    gs_send, gs_recv, ln_send, ln_recv,
):
    G, V, T, S, H, C, CW, RP, LAG = sizes
    NC = H * C
    VS = V * S
    g, v, t, s = (lax.axis_index(a) for a in ("groups", "vocab", "tokens", "section"))
    me = v * S + s
    rows = th.shape[0]
    R = rows // H
    fc = th.shape[1] // C
    F = sw.shape[0]
    half = F // 2
    wc = half // CW
    frames, DS = sh.shape
    N = tw.shape[1]
    w = DS // VS
    per = V // T
    rp = frames // RP

    def did(gg=None, vv=None, tt=None, ss=None):
        pick = lambda a, b: b if a is None else a
        return (pick(gg, g), pick(vv, v), pick(tt, t), pick(ss, s))

    def remote(src, dst, send, recv, where):
        return pltpu.make_async_remote_copy(
            src_ref=src, dst_ref=dst, send_sem=send, recv_sem=recv,
            device_id=where, device_id_type=MESH,
        )

    def vs_peer(k):
        other = lax.rem(me + k, VS)
        return did(vv=other // S, ss=lax.rem(other, S)), other

    def each(lo, hi, body):
        def run(i, carry):
            body(i)
            return carry
        lax.fori_loop(lo, hi, run, 0)

    barrier = pltpu.get_barrier_semaphore()

    def greet(where):
        pl.semaphore_signal(barrier, inc=1, device_id=where, device_id_type=MESH)

    loads = [
        pltpu.make_async_copy(source, target, in_sem.at[i])
        for i, (source, target) in enumerate(
            ((sh_in, sh), (gain_in, gain), (labels_in, labels), (align_in, align), (mask_in, mask))
        )
    ]
    for load in loads:
        load.start()
    def th_at(cc):
        h, c = cc // C, cc % C
        return th.at[h * R:(h + 1) * R, c * fc:(c + 1) * fc]

    for c in range(C):
        pltpu.make_async_copy(tw.at[c * fc:(c + 1) * fc], twv.at[c], tw_sem).start()
    for cc in range(NC):
        pltpu.make_async_copy(th_at(cc), tbuf.at[cc, me], own_sem).start()
    sw_copy = pltpu.make_async_copy(sw, wbuf.at[pl.ds(pl.multiple_of(t * F, F), F)], sw_sem)
    sw_copy.start()

    each(1, VS, lambda k: greet(vs_peer(k)[0]))
    each(1, T, lambda k: greet(did(tt=lax.rem(t + k, T))))
    greet(did(gg=1 - g))
    pl.semaphore_wait(barrier, VS - 1 + T - 1 + 1)

    def go_left(o, c, src):
        return remote(src, tbuf.at[c, o * S + s], left_send.at[o], z_recv.at[o, c], did(vv=v - 1))

    def go_right(o, c, src):
        return remote(src, tbuf.at[c, o * S + s], right_send.at[o], z_recv.at[o, c], did(vv=v + 1))

    def go_sib(o, c, src):
        return remote(src, tbuf.at[c, o * S + s], sib_send.at[o], s_recv.at[o, c], did(ss=1 - s))

    for cc in range(NC):
        @pl.when(v > 0)
        def _():
            go_left(v, cc, th_at(cc)).start()

        @pl.when(v < V - 1)
        def _():
            go_right(v, cc, th_at(cc)).start()

    def w_at(tt, hh, cw):
        return wbuf.at[pl.ds(pl.multiple_of(tt * F + hh * half + cw * wc, wc), wc)]

    def go_x(k, cw):
        to = lax.rem(t + k, T)
        src = sw.at[pl.ds(pl.multiple_of(g * half + cw * wc, wc), wc)]
        return remote(src, w_at(t, g, cw), x_send.at[to], x_recv.at[t, cw], did(tt=to))

    def go_y(tt, cw):
        return remote(w_at(tt, g, cw), w_at(tt, g, cw), y_send.at[tt], y_recv.at[tt], did(gg=1 - g))

    def x_wait(tt, cw):
        remote(w_at(tt, g, cw), w_at(tt, g, cw), x_send.at[tt], x_recv.at[tt, cw], did(tt=tt)).wait_recv()

    def w_half(tt, hh):
        return wbuf.at[pl.ds(pl.multiple_of(tt * F + hh * half, half), half)]

    def all_x(k):
        to = lax.rem(t + k, T)
        return remote(w_half(t, g), w_half(t, g), x_send.at[to], x_recv.at[t, 0], did(tt=to))

    def all_y(k, hh):
        tt = lax.rem(t + k, T)
        return remote(w_half(tt, hh), w_half(tt, hh), y_send.at[tt], y_recv.at[tt], did(gg=1 - g))

    nev = (T - 1) * CW
    each(0, nev, lambda j: go_x(j // CW + 1, lax.rem(j, CW)).start())
    for cc in range(NC):
        go_sib(v, cc, th_at(cc)).start()

    def pass_on(j):
        tt = lax.rem(t + T - 1 - j // CW, T)
        cw = lax.rem(j, CW)
        x_wait(tt, cw)
        go_y(tt, cw).start()

    for load in loads:
        load.wait()
    hid = sh[...].astype(jnp.float32)
    inverse = lax.rsqrt(jnp.mean(hid * hid, axis=1, keepdims=True) + epsilon)
    normed[...] = (hid * inverse * gain[...]).astype(jnp.bfloat16)

    def multiply(o, cc):
        x = tbuf[cc, pl.ds(o * S, S)].reshape(S * R, fc)
        acc[o, cc // C] += jnp.dot(x, twv[lax.rem(cc, C)], preferred_element_type=jnp.float32)

    def go_acc(o, h):
        p = lax.rem(o, per)
        return remote(acc.at[o, h], tin.at[t, p, h], acc_send.at[o], acc_recv.at[t], did(tt=o // per))

    def finished(o, cc):
        @pl.when((lax.rem(cc, C) == C - 1) & (o // per != t))
        def _():
            go_acc(o, cc // C).start()

    acc[...] = jnp.zeros_like(acc)

    pltpu.make_async_copy(tbuf.at[:, me], tbuf.at[:, me], own_sem).wait()
    pltpu.make_async_copy(twv, twv, tw_sem).wait()

    def own_chunk(c):
        other = tbuf.at[c, v * S + 1 - s]
        remote(other, other, sib_send.at[v], s_recv.at[v, c], did(ss=1 - s)).wait_recv()
        multiply(v, c)
        finished(v, c)

    each(0, NC, own_chunk)

    def take(o, c, onward, has_next):
        here = tbuf.at[c, o * S + s]
        remote(here, here, sib_send.at[o], z_recv.at[o, c], did(ss=1 - s)).wait_recv()

        @pl.when(has_next)
        def _():
            onward(o, c, here).start()

        go_sib(o, c, here).start()

    def use(o, c):
        other = tbuf.at[c, o * S + 1 - s]
        remote(other, other, sib_send.at[o], s_recv.at[o, c], did(ss=1 - s)).wait_recv()
        multiply(o, c)
        finished(o, c)

    steps = (V - 1) * NC
    stride = max(1, (steps - 2) // nev)

    def step(i):
        k, c = i // NC + 1, lax.rem(i, NC)

        @pl.when(i < steps)
        def _():
            @pl.when(v + k < V)
            def _():
                take(v + k, c, go_left, v > 0)

            @pl.when(v - k >= 0)
            def _():
                take(v - k, c, go_right, v < V - 1)

        j = i // stride - 1

        @pl.when((lax.rem(i, stride) == 0) & (j >= 0) & (j < nev))
        def _():
            pass_on(j)

        @pl.when(i > 0)
        def _():
            kk, cc = (i - 1) // NC + 1, lax.rem(i - 1, NC)

            @pl.when(v + kk < V)
            def _():
                use(v + kk, cc)

            @pl.when(v - kk >= 0)
            def _():
                use(v - kk, cc)

    each(0, steps + 1, step)
    each(min(nev, steps // stride), nev, pass_on)

    sw_copy.wait()

    each(1, T, lambda k: all_y(k, 1 - g).wait_recv())
    student = jnp.dot(normed[...], wbuf[...], preferred_element_type=jnp.float32)
    lane_n = lax.broadcasted_iota(jnp.int32, (frames, N), 1)
    lane = lax.broadcasted_iota(jnp.int32, (frames, frames), 1)
    sub = lax.broadcasted_iota(jnp.int32, (frames, frames), 0)

    def to_columns(row):
        return jnp.transpose(jnp.broadcast_to(row, (frames, frames)))

    label_col = to_columns(labels[...].astype(jnp.float32)).astype(jnp.int32)[:, 0:1]
    onehot = (label_col - me * N) == lane_n
    label_logit = jnp.sum(jnp.where(onehot, student, 0.0), axis=1, keepdims=True)
    top_s = jnp.max(student, axis=1, keepdims=True)
    sum_s = jnp.sum(jnp.exp(student - top_s), axis=1, keepdims=True)
    align_cols = to_columns(align[...].astype(jnp.float32)).astype(jnp.int32) - t * frames
    pick = (align_cols == lane).astype(jnp.bfloat16)

    def tin_wait(k):
        tt = lax.rem(t + k, T)
        remote(tin.at[tt], tin.at[tt], acc_send.at[0], acc_recv.at[tt], did(tt=tt)).wait_recv()

    each(1, T, tin_wait)
    for p in range(per):
        for h in range(H):
            total = acc[t * per + p, h]
            for k in range(1, T):
                total = total + tin[lax.rem(t + k, T), p, h]
            for ss in range(S):
                at = (p * S + ss) * rows + h * R
                bl[at:at + R, :] = total[ss * R:(ss + 1) * R]
    whole = bl[...]
    hi = whole.astype(jnp.bfloat16)
    rest = whole - hi.astype(jnp.float32)
    mid = rest.astype(jnp.bfloat16)
    low = (rest - mid.astype(jnp.float32)).astype(jnp.bfloat16)
    rows_of = lambda piece: jnp.dot(pick, piece, preferred_element_type=jnp.float32)
    aligned = (rows_of(low) + rows_of(mid)) + rows_of(hi)
    top_t = jnp.max(aligned, axis=1, keepdims=True)
    exp_t = jnp.exp(aligned - top_t)
    sum_t = jnp.sum(exp_t, axis=1, keepdims=True)
    cross_t = jnp.sum(exp_t * (aligned - student), axis=1, keepdims=True)

    packed = jnp.zeros((frames, frames), jnp.float32)
    for i, column in enumerate((top_t, sum_t, cross_t, top_s, sum_s, label_logit)):
        packed = jnp.where(lane == i, column, packed)
    stats[me] = jnp.transpose(packed)[0:8, :]

    def go_stat(k):
        where, other = vs_peer(k)
        return remote(stats.at[me], stats.at[me], stat_send, stat_recv, where)

    each(1, VS, lambda k: go_stat(k).start())

    def peers(buf, send, recv):
        return remote(buf.at[0:VS - 1], buf.at[0:VS - 1], send, recv, did(ss=1 - s))

    peers(stats, stat_send, stat_recv).wait_recv()
    st = stats[...]
    row = lambda i: st[:, i, :]
    all_t = jnp.max(row(0), axis=0, keepdims=True)
    all_s = jnp.max(row(3), axis=0, keepdims=True)
    scale_t = jnp.exp(row(0) - all_t)
    scale_s = jnp.exp(row(3) - all_s)
    add = lambda x: jnp.sum(x, axis=0, keepdims=True)
    total_t = add(row(1) * scale_t)
    lse_t = all_t + jnp.log(total_t)
    lse_s = all_s + jnp.log(add(row(4) * scale_s))
    diverge = add(row(2) * scale_t) / total_t - lse_t + lse_s
    cross_term = lse_s - add(row(5))
    mask_float = mask[...].astype(jnp.float32)
    mask_count = jnp.sum(jnp.sum(mask_float, axis=1, keepdims=True), axis=0, keepdims=True)
    own_mask = mask[pl.ds(t, 1), :].astype(jnp.float32)
    row_weight = own_mask * (T * frames) / mask_count
    rl_out[...] = row_weight * (diverge + label_weight * cross_term)

    unpacked = jnp.where(sub == 0, lse_t, jnp.where(sub == 1, lse_s, row_weight))
    columns = jnp.transpose(unpacked)
    teacher_prob = jnp.exp(aligned - columns[:, 0:1])
    student_prob = jnp.exp(student - columns[:, 1:2])
    grad = (
        loss_scale * columns[:, 2:3]
        * ((1.0 + label_weight) * student_prob - teacher_prob - label_weight * onehot.astype(jnp.float32))
    ).astype(jnp.bfloat16)
    lg_out[...] = grad
    stores = [
        pltpu.make_async_copy(source, target, out_sem.at[i])
        for i, (source, target) in enumerate((
            (rl_out, rl_hbm),
            (lg_out, out_hbm.at[:, 0:N]),
            (hg_out, out_hbm.at[:, N:]),
        ))
    ]
    stores[0].start()
    stores[1].start()

    inner_acc[...] = jnp.zeros_like(inner_acc)

    def term(block):
        at = pl.multiple_of(block * w, w)
        value = lax.dot_general(
            lg_out[...], wbuf[pl.ds(at, w), :], (((1,), (1,)), ((), ())), preferred_element_type=jnp.float32
        )
        weighted = value * gain[:, pl.ds(at, w)] * sh[:, pl.ds(at, w)].astype(jnp.float32)
        inner_acc[...] += jnp.sum(weighted, axis=1, keepdims=True)
        return value

    def go_gs(b):
        return remote(sibout.at[b], sibin.at[b], gs_send, gs_recv.at[b], did(ss=1 - s))

    def order(q):
        return lax.rem(q, 2) * (q // 2) + (1 - lax.rem(q, 2)) * (V - 1 - q // 2)

    def for_sib(q):
        b = order(q)
        sibout[b] = term(b * S + 1 - s)
        go_gs(b).start()

    def for_own(q):
        b = order(q)
        part[b] = term(b * S + s)

    def piece(buf, b, p):
        return buf.at[b, pl.ds(pl.multiple_of(p * rp, rp), rp)]

    def go_line(buf, turn, b, p, onward):
        return remote(piece(part, b, p), piece(buf, b, p), ln_send, ln_recv.at[b + turn, p], did(vv=onward))

    def line(n, buf, turn, b_of, comes, onward):
        q, p = n // RP, lax.rem(n, RP)
        b = b_of(q)

        @pl.when(p == 0)
        def _():
            go_gs(b).wait_recv()
            part[b] += sibin[b]

        @pl.when(comes)
        def _():
            at = pl.ds(pl.multiple_of(p * rp, rp), rp)
            go_line(buf, turn, b, p, onward).wait_recv()
            part[b, at] += buf[b, at]

        go_line(buf, turn, b, p, onward).start()

    from_top, from_zero = (lambda q: V - 1 - q), (lambda q: q)

    def line_step(i):
        n = i - v * LAG

        @pl.when((n >= 0) & (n < (V - 1 - v) * RP))
        def _():
            line(n, rin, 1, from_top, v > 0, v + 1)

        m = i - (V - 1 - v) * LAG

        @pl.when((m >= 0) & (m < v * RP))
        def _():
            line(m, lin, 0, from_zero, v < V - 1, v - 1)

    each(0, 2, for_sib)
    each(0, 2, for_own)
    each(0, LAG, line_step)
    each(2, V, for_sib)
    each(2, V, for_own)
    inner_in[me] = jnp.transpose(jnp.broadcast_to(inner_acc[...], (frames, frames)))[0:8, :]

    def go_inner(k):
        where, other = vs_peer(k)
        return remote(inner_in.at[me], inner_in.at[me], inner_send, inner_recv, where)

    each(1, VS, lambda k: go_inner(k).start())
    each(LAG, (V - 1) * max(RP, LAG), line_step)

    def sent(o):
        here = tbuf.at[:, o * S + s]

        @pl.when((o >= v) & (v > 0))
        def _():
            remote(here, here, left_send.at[o], z_recv.at[o, 0], did(vv=v - 1)).wait_send()

        @pl.when((o <= v) & (v < V - 1))
        def _():
            remote(here, here, right_send.at[o], z_recv.at[o, 0], did(vv=v + 1)).wait_send()

        remote(here, here, sib_send.at[o], s_recv.at[o, 0], did(ss=1 - s)).wait_send()

        @pl.when(o // per != t)
        def _():
            remote(acc.at[o], acc.at[o], acc_send.at[o], acc_recv.at[t], did(tt=o // per)).wait_send()

    each(0, V, sent)

    def w_sent(k):
        all_x(k).wait_send()
        all_y(k, g).wait_send()

    each(1, T, w_sent)
    remote(sibout, sibout, gs_send, gs_recv.at[0], did(ss=1 - s)).wait_send()
    peers(stats, stat_send, stat_recv).wait_send()
    peers(inner_in, inner_send, inner_recv).wait_send()
    peers(inner_in, inner_send, inner_recv).wait_recv()
    inner_total = jnp.sum(inner_in[...], axis=0)[0:1, :]
    inner_rows = to_columns(inner_total)[:, 0:1]

    go_gs(v).wait_recv()
    part[v] += sibin[v]

    def last(buf, turn, onward):
        each(0, RP, lambda p: go_line(buf, turn, v, p, onward).wait_recv())
        part[v] += buf[v]

    @pl.when(v > 0)
    def _():
        last(rin, 1, v - 1)

    @pl.when(v < V - 1)
    def _():
        last(lin, 0, v + 1)

    mine = pl.multiple_of(me * w, w)
    scaled = part[v] * gain[:, pl.ds(mine, w)]
    own_hidden = sh[:, pl.ds(mine, w)].astype(jnp.float32)
    hg_out[...] = (inverse * scaled - own_hidden * (inverse**3 * inner_rows / DS)).astype(jnp.bfloat16)

    stores[2].start()

    some = part.at[0:V - 1]
    remote(some, some, ln_send, ln_recv.at[0, 0], did(ss=1 - s)).wait_send()
    for store in stores:
        store.wait()


def spread(loss_in, both_in, loss_hbm, grad_hbm, hidden_hbm, loss, grad, hidden, sem):
    N = grad.shape[1]
    loads = [
        pltpu.make_async_copy(source, target, sem.at[i])
        for i, (source, target) in enumerate(
            ((both_in.at[:, 0:N], grad), (both_in.at[:, N:], hidden), (loss_in, loss))
        )
    ]
    stores = [
        pltpu.make_async_copy(source, target, sem.at[i])
        for i, (source, target) in enumerate(((grad, grad_hbm), (hidden, hidden_hbm), (loss, loss_hbm)))
    ]
    for load in loads:
        load.start()
    for load, store in zip(loads, stores):
        load.wait()
        store.start()
    for store in stores:
        store.wait()


def local(sizes, teacher_hidden, teacher_weight, student_hidden, student_gain, student_weight, labels, alignment, loss_mask):
    G, V, T, S, H, C, CW, RP, LAG = sizes
    VS = V * S
    NC = H * C
    rows, width = teacher_hidden.shape
    R = rows // H
    fc = width // C
    N = teacher_weight.shape[1]
    frames, DS = student_hidden.shape
    w = DS // VS
    per = V // T
    f32, bf16 = jnp.float32, jnp.bfloat16
    dma = pltpu.SemaphoreType.DMA
    hbm = pl.BlockSpec(memory_space=pl.ANY)
    row_loss, both = pl.pallas_call(
        functools.partial(kernel, sizes),
        out_shape=(jax.ShapeDtypeStruct((1, frames), f32), jax.ShapeDtypeStruct((frames, N + w), bf16)),
        in_specs=[hbm] * 8,
        out_specs=(hbm, hbm),
        scratch_shapes=[
            pltpu.VMEM((frames, DS), bf16),
            pltpu.VMEM((1, DS), f32),
            pltpu.VMEM((1, frames), jnp.int32),
            pltpu.VMEM((1, frames), jnp.int32),
            pltpu.VMEM((T, frames), jnp.int32),
            pltpu.VMEM((1, frames), f32),
            pltpu.VMEM((frames, N), bf16),
            pltpu.VMEM((frames, w), bf16),
            pltpu.VMEM((NC, VS, R, fc), bf16),
            pltpu.VMEM((C, fc, N), bf16),
            pltpu.VMEM((DS, N), bf16),
            pltpu.VMEM((frames, DS), bf16),
            pltpu.VMEM((V, H, S * R, N), f32),
            pltpu.VMEM((T, per, H, S * R, N), f32),
            pltpu.VMEM((frames, N), f32),
            pltpu.VMEM((VS, 8, frames), f32),
            pltpu.VMEM((VS, 8, frames), f32),
            pltpu.VMEM((V, frames, w), f32),
            pltpu.VMEM((V, frames, w), f32),
            pltpu.VMEM((V, frames, w), f32),
            pltpu.VMEM((V, frames, w), f32),
            pltpu.VMEM((V, frames, w), f32),
            pltpu.VMEM((frames, 1), f32),
            dma, dma, dma, dma((5,)), dma((3,)),
            dma((V,)), dma((V,)), dma((V,)), dma((V, NC)), dma((V, NC)),
            dma((T,)), dma((T, CW)), dma((T,)), dma((T,)),
            dma((V,)), dma((T,)),
            dma, dma, dma, dma,
            dma, dma((V,)), dma, dma((V + 1, RP)),
        ],
        compiler_params=pltpu.CompilerParams(
            collective_id=0, has_side_effects=True, vmem_limit_bytes=63 * 2**20
        ),
    )(
        teacher_hidden, teacher_weight, student_hidden, student_gain.reshape(1, DS), student_weight,
        labels.reshape(1, frames), alignment.reshape(1, frames), loss_mask.reshape(T, frames),
    )
    row_loss, logit_grad, hidden_grad = pl.pallas_call(
        spread,
        out_shape=(
            jax.ShapeDtypeStruct((1, frames), f32),
            jax.ShapeDtypeStruct((frames, N), bf16),
            jax.ShapeDtypeStruct((frames, w), bf16),
        ),
        in_specs=[hbm] * 2,
        out_specs=(hbm,) * 3,
        scratch_shapes=[pltpu.VMEM((1, frames), f32), pltpu.VMEM((frames, N), bf16), pltpu.VMEM((frames, w), bf16), dma((3,))],
    )(row_loss, both)
    return row_loss.reshape(frames), logit_grad, hidden_grad


def solution(mesh):
    sizes = tuple(mesh.shape[a] for a in ("groups", "vocab", "tokens", "section")) + (2, 2, 4, 4, 2)
    in_specs = (
        P(("groups", "vocab", "section"), "tokens"),
        P("tokens", ("vocab", "section")),
        P(("groups", "tokens"), None),
        P(),
        P("tokens", ("vocab", "section")),
        P(("groups", "tokens")),
        P(("groups", "tokens")),
        P("groups"),
    )
    out_specs = (
        P(("groups", "tokens")),
        P(("groups", "tokens"), ("vocab", "section")),
        P(("groups", "tokens"), ("vocab", "section")),
    )
    return jax.shard_map(
        functools.partial(local, sizes), mesh=mesh, in_specs=in_specs, out_specs=out_specs, check_vma=False
    )
```

```python
import functools

import jax
import jax.numpy as jnp
from jax import lax
from jax.experimental import pallas as pl
from jax.experimental.pallas import tpu as pltpu
from jax.sharding import PartitionSpec as P

label_weight = 0.2
loss_scale = 16.0
epsilon = 1e-05
MESH = pl.DeviceIdType.MESH


def kernel(
    sizes, th, tw, sh_in, gain_in, sw, labels_in, align_in, mask_in,
    rl_hbm, out_hbm,
    sh, gain, labels, align, mask, rl_out, lg_out, hg_out,
    tbuf, twv, wbuf, normed, acc, tin, bl, stats, inner_in, sibout, sibin, part, rin, lin, student_ref, packed,
    tw_sem, own_sem, sw_sem, in_sem, out_sem,
    left_send, right_send, sib_send, z_recv, s_recv,
    x_send, x_recv, y_send, y_recv,
    acc_send, acc_recv,
    stat_send, stat_recv, inner_send, inner_recv,
    gs_send, gs_recv, ln_send, ln_recv,
):
    G, V, T, S, H, C, CW, RP, LAG, M = sizes
    NC = H * C
    VS = V * S
    M = M if T == 2 and V > 2 else NC
    g, v, t, s = (lax.axis_index(a) for a in ("groups", "vocab", "tokens", "section"))
    me = v * S + s
    rows = th.shape[0]
    R = rows // H
    fc = th.shape[1] // C
    F = sw.shape[0]
    half = F // 2
    wc = half // CW
    frames, DS = sh.shape
    N = tw.shape[1]
    w = DS // VS
    per = V // T
    rp = frames // RP

    def did(gg=None, vv=None, tt=None, ss=None):
        pick = lambda a, b: b if a is None else a
        return (pick(gg, g), pick(vv, v), pick(tt, t), pick(ss, s))

    def remote(src, dst, send, recv, where):
        return pltpu.make_async_remote_copy(
            src_ref=src, dst_ref=dst, send_sem=send, recv_sem=recv,
            device_id=where, device_id_type=MESH,
        )

    def vs_peer(k):
        other = lax.rem(me + k, VS)
        return did(vv=other // S, ss=lax.rem(other, S)), other

    def each(lo, hi, body):
        def run(i, carry):
            body(i)
            return carry
        lax.fori_loop(lo, hi, run, 0)

    barrier = pltpu.get_barrier_semaphore()

    def greet(where):
        pl.semaphore_signal(barrier, inc=1, device_id=where, device_id_type=MESH)

    loads = [
        pltpu.make_async_copy(source, target, in_sem.at[i])
        for i, (source, target) in enumerate(
            ((sh_in, sh), (gain_in, gain), (labels_in, labels), (align_in, align), (mask_in, mask))
        )
    ]
    for load in loads:
        load.start()
    def th_at(cc):
        h, c = cc // C, cc % C
        return th.at[h * R:(h + 1) * R, c * fc:(c + 1) * fc]

    for c in range(C):
        pltpu.make_async_copy(tw.at[c * fc:(c + 1) * fc], twv.at[c], tw_sem).start()
    for cc in range(NC):
        pltpu.make_async_copy(th_at(cc), tbuf.at[cc, me], own_sem).start()
    sw_copy = pltpu.make_async_copy(sw, wbuf.at[pl.ds(pl.multiple_of(t * F, F), F)], sw_sem)
    sw_copy.start()

    each(1, VS, lambda k: greet(vs_peer(k)[0]))
    each(1, T, lambda k: greet(did(tt=lax.rem(t + k, T))))
    greet(did(gg=1 - g))
    pl.semaphore_wait(barrier, VS - 1 + T - 1 + 1)

    def go_left(o, c, src):
        return remote(src, tbuf.at[c, o * S + s], left_send.at[o], z_recv.at[o, c], did(vv=v - 1))

    def go_right(o, c, src):
        return remote(src, tbuf.at[c, o * S + s], right_send.at[o], z_recv.at[o, c], did(vv=v + 1))

    def go_sib(o, c, src):
        return remote(src, tbuf.at[c, o * S + s], sib_send.at[o], s_recv.at[o, c], did(ss=1 - s))

    late_left = (v == 1) & (t == 0)
    late_right = (v == V - 2) & (t == T - 1)

    def send_own(lo, hi, to_left, to_right):
        for cc in range(lo, hi):
            @pl.when(to_left)
            def _():
                go_left(v, cc, th_at(cc)).start()

            @pl.when(to_right)
            def _():
                go_right(v, cc, th_at(cc)).start()

    send_own(0, M, v > 0, v < V - 1)
    send_own(M, NC, (v > 0) & jnp.logical_not(late_left), (v < V - 1) & jnp.logical_not(late_right))

    def w_at(tt, hh, cw):
        return wbuf.at[pl.ds(pl.multiple_of(tt * F + hh * half + cw * wc, wc), wc)]

    def go_x(k, cw):
        to = lax.rem(t + k, T)
        src = sw.at[pl.ds(pl.multiple_of(g * half + cw * wc, wc), wc)]
        return remote(src, w_at(t, g, cw), x_send.at[to], x_recv.at[t, cw], did(tt=to))

    def go_y(tt, cw):
        return remote(w_at(tt, g, cw), w_at(tt, g, cw), y_send.at[tt], y_recv.at[tt], did(gg=1 - g))

    def x_wait(tt, cw):
        remote(w_at(tt, g, cw), w_at(tt, g, cw), x_send.at[tt], x_recv.at[tt, cw], did(tt=tt)).wait_recv()

    def w_half(tt, hh):
        return wbuf.at[pl.ds(pl.multiple_of(tt * F + hh * half, half), half)]

    def all_x(k):
        to = lax.rem(t + k, T)
        return remote(w_half(t, g), w_half(t, g), x_send.at[to], x_recv.at[t, 0], did(tt=to))

    def all_y(k, hh):
        tt = lax.rem(t + k, T)
        return remote(w_half(tt, hh), w_half(tt, hh), y_send.at[tt], y_recv.at[tt], did(gg=1 - g))

    nev = (T - 1) * CW
    each(0, nev, lambda j: go_x(j // CW + 1, lax.rem(j, CW)).start())
    for cc in range(NC):
        go_sib(v, cc, th_at(cc)).start()

    def pass_on(j):
        tt = lax.rem(t + T - 1 - j // CW, T)
        cw = lax.rem(j, CW)
        x_wait(tt, cw)
        go_y(tt, cw).start()

    for load in loads:
        load.wait()
    hid = sh[...].astype(jnp.float32)
    inverse = lax.rsqrt(jnp.mean(hid * hid, axis=1, keepdims=True) + epsilon)
    normed[...] = (hid * inverse * gain[...]).astype(jnp.bfloat16)

    def multiply(o, cc):
        x = tbuf[cc, pl.ds(o * S, S)].reshape(S * R, fc)
        acc[o, cc // C] += jnp.dot(x, twv[lax.rem(cc, C)], preferred_element_type=jnp.float32)

    def go_acc(o, h):
        p = lax.rem(o, per)
        return remote(acc.at[o, h], tin.at[t, p, h], acc_send.at[o], acc_recv.at[t], did(tt=o // per))

    def finished(o, cc):
        @pl.when((lax.rem(cc, C) == C - 1) & (o // per != t))
        def _():
            go_acc(o, cc // C).start()

    acc[...] = jnp.zeros_like(acc)

    pltpu.make_async_copy(tbuf.at[:, me], tbuf.at[:, me], own_sem).wait()
    pltpu.make_async_copy(twv, twv, tw_sem).wait()

    def own_chunk(c):
        other = tbuf.at[c, v * S + 1 - s]
        remote(other, other, sib_send.at[v], s_recv.at[v, c], did(ss=1 - s)).wait_recv()
        multiply(v, c)
        finished(v, c)

    each(0, NC, own_chunk)

    def take(o, c, onward, has_next):
        here = tbuf.at[c, o * S + s]
        remote(here, here, sib_send.at[o], z_recv.at[o, c], did(ss=1 - s)).wait_recv()

        @pl.when(has_next)
        def _():
            onward(o, c, here).start()

        go_sib(o, c, here).start()

    def use(o, c):
        other = tbuf.at[c, o * S + 1 - s]
        remote(other, other, sib_send.at[o], s_recv.at[o, c], did(ss=1 - s)).wait_recv()
        multiply(o, c)
        finished(o, c)

    lane_n = lax.broadcasted_iota(jnp.int32, (frames, N), 1)
    lane = lax.broadcasted_iota(jnp.int32, (frames, frames), 1)
    sub = lax.broadcasted_iota(jnp.int32, (frames, frames), 0)

    def to_columns(row):
        return jnp.transpose(jnp.broadcast_to(row, (frames, frames)))

    def is_label():
        label_col = to_columns(labels[...].astype(jnp.float32)).astype(jnp.int32)[:, 0:1]
        return (label_col - me * N) == lane_n

    steps = (V - 1) * NC
    stride = max(1, min((steps - 2) // nev, 2 * NC // CW))

    passed = (V - 2) * NC
    at_least = lambda i, a: jnp.minimum(jnp.maximum(i - a + 1, 0), 1)
    turn_left = (1 - at_least(v, 1)) * (1 - at_least(t, 1))
    turn_right = at_least(v, V - 1) * at_least(t, T - 1)

    def source(i, turn):
        j = i
        if M < NC:
            j = i + turn * ((NC - M) * at_least(i, M) - (passed + NC - M) * at_least(i, M + passed))
        return j // NC + 1, lax.rem(j, NC)

    def student_head():
        sw_copy.wait()
        each(1, T, lambda k: all_y(k, 1 - g).wait_recv())
        logits = jnp.dot(normed[...], wbuf[...], preferred_element_type=jnp.float32)
        label_logit = jnp.sum(jnp.where(is_label(), logits, 0.0), axis=1, keepdims=True)
        top = jnp.max(logits, axis=1, keepdims=True)
        total = jnp.sum(jnp.exp(logits - top), axis=1, keepdims=True)
        student_ref[...] = logits
        packed[...] = jnp.where(lane == 3, top, jnp.where(lane == 4, total, jnp.where(lane == 5, label_logit, 0.0)))

    student_at = steps - 4 if nev * stride < steps - 4 else None

    def step(i):
        @pl.when(i < steps)
        def _():
            k, c = source(i, turn_left)

            @pl.when(v + k < V)
            def _():
                take(v + k, c, go_left, v > 0)

            k, c = source(i, turn_right)

            @pl.when(v - k >= 0)
            def _():
                take(v - k, c, go_right, v < V - 1)

        if M < NC:
            @pl.when(i == passed - 1)
            def _():
                send_own(M, NC, late_left, late_right)

        j = i // stride - 1

        @pl.when((lax.rem(i, stride) == 0) & (j >= 0) & (j < nev))
        def _():
            pass_on(j)

        if student_at is not None:
            @pl.when(i == student_at)
            def _():
                student_head()

        @pl.when(i > 0)
        def _():
            k, c = source(i - 1, turn_left)

            @pl.when(v + k < V)
            def _():
                use(v + k, c)

            k, c = source(i - 1, turn_right)

            @pl.when(v - k >= 0)
            def _():
                use(v - k, c)

    each(0, steps + 1, step)
    each(min(nev, steps // stride), nev, pass_on)

    if student_at is None:
        student_head()
    student = student_ref[...]
    onehot = is_label()
    align_cols = to_columns(align[...].astype(jnp.float32)).astype(jnp.int32) - t * frames
    pick = (align_cols == lane).astype(jnp.bfloat16)

    def tin_wait(k):
        tt = lax.rem(t + k, T)
        remote(tin.at[tt], tin.at[tt], acc_send.at[0], acc_recv.at[tt], did(tt=tt)).wait_recv()

    each(1, T, tin_wait)
    for p in range(per):
        for h in range(H):
            total = acc[t * per + p, h]
            for k in range(1, T):
                total = total + tin[lax.rem(t + k, T), p, h]
            for ss in range(S):
                at = (p * S + ss) * rows + h * R
                bl[at:at + R, :] = total[ss * R:(ss + 1) * R]
    whole = bl[...]
    hi = whole.astype(jnp.bfloat16)
    rest = whole - hi.astype(jnp.float32)
    mid = rest.astype(jnp.bfloat16)
    low = (rest - mid.astype(jnp.float32)).astype(jnp.bfloat16)
    rows_of = lambda piece: jnp.dot(pick, piece, preferred_element_type=jnp.float32)
    aligned = (rows_of(low) + rows_of(mid)) + rows_of(hi)
    top_t = jnp.max(aligned, axis=1, keepdims=True)
    exp_t = jnp.exp(aligned - top_t)
    sum_t = jnp.sum(exp_t, axis=1, keepdims=True)
    cross_t = jnp.sum(exp_t * (aligned - student), axis=1, keepdims=True)

    pack = packed[...]
    for i, column in enumerate((top_t, sum_t, cross_t)):
        pack = jnp.where(lane == i, column, pack)
    stats[me] = jnp.transpose(pack)[0:8, :]

    def go_stat(k):
        where, other = vs_peer(k)
        return remote(stats.at[me], stats.at[me], stat_send, stat_recv, where)

    each(1, VS, lambda k: go_stat(k).start())

    def peers(buf, send, recv):
        return remote(buf.at[0:VS - 1], buf.at[0:VS - 1], send, recv, did(ss=1 - s))

    peers(stats, stat_send, stat_recv).wait_recv()
    st = stats[...]
    row = lambda i: st[:, i, :]
    all_t = jnp.max(row(0), axis=0, keepdims=True)
    all_s = jnp.max(row(3), axis=0, keepdims=True)
    scale_t = jnp.exp(row(0) - all_t)
    scale_s = jnp.exp(row(3) - all_s)
    add = lambda x: jnp.sum(x, axis=0, keepdims=True)
    total_t = add(row(1) * scale_t)
    lse_t = all_t + jnp.log(total_t)
    lse_s = all_s + jnp.log(add(row(4) * scale_s))
    diverge = add(row(2) * scale_t) / total_t - lse_t + lse_s
    cross_term = lse_s - add(row(5))
    mask_float = mask[...].astype(jnp.float32)
    mask_count = jnp.sum(jnp.sum(mask_float, axis=1, keepdims=True), axis=0, keepdims=True)
    own_mask = mask[pl.ds(t, 1), :].astype(jnp.float32)
    row_weight = own_mask * (T * frames) / mask_count
    rl_out[...] = row_weight * (diverge + label_weight * cross_term)

    unpacked = jnp.where(sub == 0, lse_t, jnp.where(sub == 1, lse_s, row_weight))
    columns = jnp.transpose(unpacked)
    teacher_prob = jnp.exp(aligned - columns[:, 0:1])
    student_prob = jnp.exp(student - columns[:, 1:2])
    grad = (
        loss_scale * columns[:, 2:3]
        * ((1.0 + label_weight) * student_prob - teacher_prob - label_weight * onehot.astype(jnp.float32))
    ).astype(jnp.bfloat16)
    lg_out[...] = grad
    stores = [
        pltpu.make_async_copy(source, target, out_sem.at[i])
        for i, (source, target) in enumerate((
            (rl_out, rl_hbm),
            (lg_out, out_hbm.at[:, 0:N]),
            (hg_out, out_hbm.at[:, N:]),
        ))
    ]
    stores[0].start()
    stores[1].start()

    inner = jnp.sum(grad.astype(jnp.float32) * student, axis=1, keepdims=True)
    inner_in[me] = jnp.transpose(jnp.broadcast_to(inner, (frames, frames)))[0:8, :]

    def go_inner(k):
        where, other = vs_peer(k)
        return remote(inner_in.at[me], inner_in.at[me], inner_send, inner_recv, where)

    def term(block):
        at = pl.multiple_of(block * w, w)
        return lax.dot_general(
            lg_out[...], wbuf[pl.ds(at, w), :], (((1,), (1,)), ((), ())), preferred_element_type=jnp.float32
        )

    def go_gs(b):
        return remote(sibout.at[b], sibin.at[b], gs_send, gs_recv.at[b], did(ss=1 - s))

    def order(q):
        return lax.rem(q, 2) * (q // 2) + (1 - lax.rem(q, 2)) * (V - 1 - q // 2)

    def for_sib(q):
        b = order(q)
        sibout[b] = term(b * S + 1 - s)
        go_gs(b).start()

    def for_own(q):
        b = order(q)
        part[b] = term(b * S + s)

    def piece(buf, b, p):
        return buf.at[b, pl.ds(pl.multiple_of(p * rp, rp), rp)]

    def go_line(buf, turn, b, p, onward):
        return remote(piece(part, b, p), piece(buf, b, p), ln_send, ln_recv.at[b + turn, p], did(vv=onward))

    def line(n, buf, turn, b_of, comes, onward):
        q, p = n // RP, lax.rem(n, RP)
        b = b_of(q)

        @pl.when(p == 0)
        def _():
            go_gs(b).wait_recv()
            part[b] += sibin[b]

        @pl.when(comes)
        def _():
            at = pl.ds(pl.multiple_of(p * rp, rp), rp)
            go_line(buf, turn, b, p, onward).wait_recv()
            part[b, at] += buf[b, at]

        go_line(buf, turn, b, p, onward).start()

    from_top, from_zero = (lambda q: V - 1 - q), (lambda q: q)

    def line_step(i):
        n = i - v * LAG

        @pl.when((n >= 0) & (n < (V - 1 - v) * RP))
        def _():
            line(n, rin, 1, from_top, v > 0, v + 1)

        m = i - (V - 1 - v) * LAG

        @pl.when((m >= 0) & (m < v * RP))
        def _():
            line(m, lin, 0, from_zero, v < V - 1, v - 1)

    each(0, 2, for_sib)
    each(0, 2, for_own)
    each(0, LAG, line_step)
    each(2, V, for_sib)
    each(2, V, for_own)
    each(1, VS, lambda k: go_inner(k).start())
    each(LAG, (V - 1) * max(RP, LAG), line_step)

    def sent(o):
        here = tbuf.at[:, o * S + s]

        @pl.when((o >= v) & (v > 0))
        def _():
            remote(here, here, left_send.at[o], z_recv.at[o, 0], did(vv=v - 1)).wait_send()

        @pl.when((o <= v) & (v < V - 1))
        def _():
            remote(here, here, right_send.at[o], z_recv.at[o, 0], did(vv=v + 1)).wait_send()

        remote(here, here, sib_send.at[o], s_recv.at[o, 0], did(ss=1 - s)).wait_send()

        @pl.when(o // per != t)
        def _():
            remote(acc.at[o], acc.at[o], acc_send.at[o], acc_recv.at[t], did(tt=o // per)).wait_send()

    each(0, V, sent)

    def w_sent(k):
        all_x(k).wait_send()
        all_y(k, g).wait_send()

    each(1, T, w_sent)
    remote(sibout, sibout, gs_send, gs_recv.at[0], did(ss=1 - s)).wait_send()
    peers(stats, stat_send, stat_recv).wait_send()
    peers(inner_in, inner_send, inner_recv).wait_send()
    peers(inner_in, inner_send, inner_recv).wait_recv()
    inner_total = jnp.sum(inner_in[...], axis=0)[0:1, :]
    inner_rows = to_columns(inner_total)[:, 0:1]

    go_gs(v).wait_recv()
    part[v] += sibin[v]

    def last(buf, turn, onward):
        each(0, RP, lambda p: go_line(buf, turn, v, p, onward).wait_recv())
        part[v] += buf[v]

    @pl.when(v > 0)
    def _():
        last(rin, 1, v - 1)

    @pl.when(v < V - 1)
    def _():
        last(lin, 0, v + 1)

    mine = pl.multiple_of(me * w, w)
    scaled = part[v] * gain[:, pl.ds(mine, w)]
    own_hidden = sh[:, pl.ds(mine, w)].astype(jnp.float32)
    hg_out[...] = (inverse * scaled - own_hidden * (inverse**2 * inner_rows / DS)).astype(jnp.bfloat16)

    stores[2].start()

    some = part.at[0:V - 1]
    remote(some, some, ln_send, ln_recv.at[0, 0], did(ss=1 - s)).wait_send()
    for store in stores:
        store.wait()


def spread(loss_in, both_in, loss_hbm, grad_hbm, hidden_hbm, loss, grad, hidden, sem):
    N = grad.shape[1]
    loads = [
        pltpu.make_async_copy(source, target, sem.at[i])
        for i, (source, target) in enumerate(
            ((both_in.at[:, 0:N], grad), (both_in.at[:, N:], hidden), (loss_in, loss))
        )
    ]
    stores = [
        pltpu.make_async_copy(source, target, sem.at[i])
        for i, (source, target) in enumerate(((grad, grad_hbm), (hidden, hidden_hbm), (loss, loss_hbm)))
    ]
    for load in loads:
        load.start()
    for load, store in zip(loads, stores):
        load.wait()
        store.start()
    for store in stores:
        store.wait()


def local(sizes, teacher_hidden, teacher_weight, student_hidden, student_gain, student_weight, labels, alignment, loss_mask):
    G, V, T, S, H, C, CW, RP, LAG, M = sizes
    VS = V * S
    NC = H * C
    rows, width = teacher_hidden.shape
    R = rows // H
    fc = width // C
    N = teacher_weight.shape[1]
    frames, DS = student_hidden.shape
    w = DS // VS
    per = V // T
    f32, bf16 = jnp.float32, jnp.bfloat16
    dma = pltpu.SemaphoreType.DMA
    hbm = pl.BlockSpec(memory_space=pl.ANY)
    row_loss, both = pl.pallas_call(
        functools.partial(kernel, sizes),
        out_shape=(jax.ShapeDtypeStruct((1, frames), f32), jax.ShapeDtypeStruct((frames, N + w), bf16)),
        in_specs=[hbm] * 8,
        out_specs=(hbm, hbm),
        scratch_shapes=[
            pltpu.VMEM((frames, DS), bf16),
            pltpu.VMEM((1, DS), f32),
            pltpu.VMEM((1, frames), jnp.int32),
            pltpu.VMEM((1, frames), jnp.int32),
            pltpu.VMEM((T, frames), jnp.int32),
            pltpu.VMEM((1, frames), f32),
            pltpu.VMEM((frames, N), bf16),
            pltpu.VMEM((frames, w), bf16),
            pltpu.VMEM((NC, VS, R, fc), bf16),
            pltpu.VMEM((C, fc, N), bf16),
            pltpu.VMEM((DS, N), bf16),
            pltpu.VMEM((frames, DS), bf16),
            pltpu.VMEM((V, H, S * R, N), f32),
            pltpu.VMEM((T, per, H, S * R, N), f32),
            pltpu.VMEM((frames, N), f32),
            pltpu.VMEM((VS, 8, frames), f32),
            pltpu.VMEM((VS, 8, frames), f32),
            pltpu.VMEM((V, frames, w), f32),
            pltpu.VMEM((V, frames, w), f32),
            pltpu.VMEM((V, frames, w), f32),
            pltpu.VMEM((V, frames, w), f32),
            pltpu.VMEM((V, frames, w), f32),
            pltpu.VMEM((frames, N), f32),
            pltpu.VMEM((frames, frames), f32),
            dma, dma, dma, dma((5,)), dma((3,)),
            dma((V,)), dma((V,)), dma((V,)), dma((V, NC)), dma((V, NC)),
            dma((T,)), dma((T, CW)), dma((T,)), dma((T,)),
            dma((V,)), dma((T,)),
            dma, dma, dma, dma,
            dma, dma((V,)), dma, dma((V + 1, RP)),
        ],
        compiler_params=pltpu.CompilerParams(
            collective_id=0, has_side_effects=True, vmem_limit_bytes=63 * 2**20
        ),
    )(
        teacher_hidden, teacher_weight, student_hidden, student_gain.reshape(1, DS), student_weight,
        labels.reshape(1, frames), alignment.reshape(1, frames), loss_mask.reshape(T, frames),
    )
    row_loss, logit_grad, hidden_grad = pl.pallas_call(
        spread,
        out_shape=(
            jax.ShapeDtypeStruct((1, frames), f32),
            jax.ShapeDtypeStruct((frames, N), bf16),
            jax.ShapeDtypeStruct((frames, w), bf16),
        ),
        in_specs=[hbm] * 2,
        out_specs=(hbm,) * 3,
        scratch_shapes=[pltpu.VMEM((1, frames), f32), pltpu.VMEM((frames, N), bf16), pltpu.VMEM((frames, w), bf16), dma((3,))],
    )(row_loss, both)
    return row_loss.reshape(frames), logit_grad, hidden_grad


def solution(mesh):
    sizes = tuple(mesh.shape[a] for a in ("groups", "vocab", "tokens", "section")) + (2, 4, 8, 4, 2, 3)
    in_specs = (
        P(("groups", "vocab", "section"), "tokens"),
        P("tokens", ("vocab", "section")),
        P(("groups", "tokens"), None),
        P(),
        P("tokens", ("vocab", "section")),
        P(("groups", "tokens")),
        P(("groups", "tokens")),
        P("groups"),
    )
    out_specs = (
        P(("groups", "tokens")),
        P(("groups", "tokens"), ("vocab", "section")),
        P(("groups", "tokens"), ("vocab", "section")),
    )
    return jax.shard_map(
        functools.partial(local, sizes), mesh=mesh, in_specs=in_specs, out_specs=out_specs, check_vma=False
    )
```

```python
import functools

import jax
import jax.numpy as jnp
from jax import lax
from jax.experimental import pallas as pl
from jax.experimental.pallas import tpu as pltpu
from jax.sharding import PartitionSpec as P

label_weight = 0.2
loss_scale = 16.0
epsilon = 1e-05
MESH = pl.DeviceIdType.MESH


def kernel(
    sizes, th, tw, sh_in, gain_in, sw, labels_in, align_in, mask_in,
    rl_hbm, out_hbm,
    sh, gain, labels, align, mask, rl_out, lg_out, hg_out,
    tbuf, twv, wbuf, normed, acc, tin, bl, stats, inner_in, sibout, sibin, part, rin, lin, student_ref, packed,
    tw_sem, own_sem, sw_sem, in_sem, out_sem,
    left_send, right_send, sib_send, z_recv, s_recv,
    x_send, x_recv, y_send, y_recv,
    acc_send, acc_recv,
    stat_send, stat_recv, inner_send, inner_recv,
    gs_send, gs_recv, ln_send, ln_recv,
):
    G, V, T, S, H, C, CW, RP, LAG, M, OWN = sizes
    NC = H * C
    VS = V * S
    M = M if T == 2 and V > 2 else NC
    g, v, t, s = (lax.axis_index(a) for a in ("groups", "vocab", "tokens", "section"))
    me = v * S + s
    rows = th.shape[0]
    R = rows // H
    fc = th.shape[1] // C
    F = sw.shape[0]
    half = F // 2
    wc = half // CW
    frames, DS = sh.shape
    N = tw.shape[1]
    w = DS // VS
    per = V // T
    rp = frames // RP

    def did(gg=None, vv=None, tt=None, ss=None):
        pick = lambda a, b: b if a is None else a
        return (pick(gg, g), pick(vv, v), pick(tt, t), pick(ss, s))

    def remote(src, dst, send, recv, where):
        return pltpu.make_async_remote_copy(
            src_ref=src, dst_ref=dst, send_sem=send, recv_sem=recv,
            device_id=where, device_id_type=MESH,
        )

    def vs_peer(k):
        other = lax.rem(me + k, VS)
        return did(vv=other // S, ss=lax.rem(other, S)), other

    def each(lo, hi, body):
        def run(i, carry):
            body(i)
            return carry
        lax.fori_loop(lo, hi, run, 0)

    barrier = pltpu.get_barrier_semaphore()

    def greet(where):
        pl.semaphore_signal(barrier, inc=1, device_id=where, device_id_type=MESH)

    loads = [
        pltpu.make_async_copy(source, target, in_sem.at[i])
        for i, (source, target) in enumerate(
            ((sh_in, sh), (gain_in, gain), (labels_in, labels), (align_in, align), (mask_in, mask))
        )
    ]
    for load in loads:
        load.start()
    def th_at(cc):
        h, c = cc // C, cc % C
        return th.at[h * R:(h + 1) * R, c * fc:(c + 1) * fc]

    for c in range(C):
        pltpu.make_async_copy(tw.at[c * fc:(c + 1) * fc], twv.at[c], tw_sem).start()
    for cc in range(NC):
        pltpu.make_async_copy(th_at(cc), tbuf.at[cc, me], own_sem).start()
    sw_copy = pltpu.make_async_copy(sw, wbuf.at[pl.ds(pl.multiple_of(t * F, F), F)], sw_sem)
    sw_copy.start()

    each(1, VS, lambda k: greet(vs_peer(k)[0]))
    each(1, T, lambda k: greet(did(tt=lax.rem(t + k, T))))
    greet(did(gg=1 - g))
    pl.semaphore_wait(barrier, VS - 1 + T - 1 + 1)

    def go_left(o, c, src):
        return remote(src, tbuf.at[c, o * S + s], left_send.at[o], z_recv.at[o, c], did(vv=v - 1))

    def go_right(o, c, src):
        return remote(src, tbuf.at[c, o * S + s], right_send.at[o], z_recv.at[o, c], did(vv=v + 1))

    def go_sib(o, c, src):
        return remote(src, tbuf.at[c, o * S + s], sib_send, s_recv.at[o, c], did(ss=1 - s))

    late_left = (v == 1) & (t == 0)
    late_right = (v == V - 2) & (t == T - 1)

    def send_own(lo, hi, to_left, to_right):
        for cc in range(lo, hi):
            @pl.when(to_left)
            def _():
                go_left(v, cc, th_at(cc)).start()

            @pl.when(to_right)
            def _():
                go_right(v, cc, th_at(cc)).start()

    send_own(0, M, v > 0, v < V - 1)
    send_own(M, NC, (v > 0) & jnp.logical_not(late_left), (v < V - 1) & jnp.logical_not(late_right))

    def w_at(tt, hh, cw):
        return wbuf.at[pl.ds(pl.multiple_of(tt * F + hh * half + cw * wc, wc), wc)]

    def go_x(k, cw):
        to = lax.rem(t + k, T)
        src = sw.at[pl.ds(pl.multiple_of(g * half + cw * wc, wc), wc)]
        return remote(src, w_at(t, g, cw), x_send.at[to], x_recv.at[k - 1, cw], did(tt=to))

    def go_y(tt, cw):
        return remote(w_at(tt, g, cw), w_at(tt, g, cw), y_send.at[tt], y_recv.at[tt], did(gg=1 - g))

    def x_wait(k, tt, cw):
        remote(w_at(tt, g, cw), w_at(tt, g, cw), x_send.at[tt], x_recv.at[k - 1, cw], did(tt=tt)).wait_recv()

    def w_half(tt, hh):
        return wbuf.at[pl.ds(pl.multiple_of(tt * F + hh * half, half), half)]

    def all_x(k):
        to = lax.rem(t + k, T)
        return remote(w_half(t, g), w_half(t, g), x_send.at[to], x_recv.at[0, 0], did(tt=to))

    def all_y(k, hh):
        tt = lax.rem(t + k, T)
        return remote(w_half(tt, hh), w_half(tt, hh), y_send.at[tt], y_recv.at[tt], did(gg=1 - g))

    nev = (T - 1) * CW
    each(0, nev, lambda j: go_x(j // CW + 1, lax.rem(j, CW)).start())
    for cc in range(NC):
        go_sib(v, cc, th_at(cc)).start()

    def pass_on(j):
        tt = lax.rem(t + T - 1 - j // CW, T)
        cw = lax.rem(j, CW)
        x_wait(j // CW + 1, tt, cw)
        go_y(tt, cw).start()

    for load in loads:
        load.wait()
    hid = sh[...].astype(jnp.float32)
    inverse = lax.rsqrt(jnp.mean(hid * hid, axis=1, keepdims=True) + epsilon)
    normed[...] = (hid * inverse * gain[...]).astype(jnp.bfloat16)

    def multiply(o, cc):
        x = tbuf[cc, pl.ds(o * S, S)].reshape(S * R, fc)
        acc[o, cc // C] += jnp.dot(x, twv[lax.rem(cc, C)], preferred_element_type=jnp.float32)

    def go_acc(o, h):
        p = lax.rem(o, per)
        return remote(acc.at[o, h], tin.at[t, p, h], acc_send, acc_recv.at[t], did(tt=o // per))

    def finished(o, cc):
        @pl.when((lax.rem(cc, C) == C - 1) & (o // per != t))
        def _():
            go_acc(o, cc // C).start()

    acc[...] = jnp.zeros_like(acc)

    pltpu.make_async_copy(tbuf.at[:, me], tbuf.at[:, me], own_sem).wait()
    pltpu.make_async_copy(twv, twv, tw_sem).wait()

    def own_chunk(c):
        other = tbuf.at[c, v * S + 1 - s]
        remote(other, other, sib_send, s_recv.at[v, c], did(ss=1 - s)).wait_recv()
        multiply(v, c)
        finished(v, c)

    spread_own = V > 2
    if not spread_own:
        each(0, NC, own_chunk)

    def take(o, c, onward, has_next):
        here = tbuf.at[c, o * S + s]
        remote(here, here, sib_send, z_recv.at[o, c], did(ss=1 - s)).wait_recv()

        @pl.when(has_next)
        def _():
            onward(o, c, here).start()

        go_sib(o, c, here).start()

    def use(o, c):
        other = tbuf.at[c, o * S + 1 - s]
        remote(other, other, sib_send, s_recv.at[o, c], did(ss=1 - s)).wait_recv()
        multiply(o, c)
        finished(o, c)

    lane_n = lax.broadcasted_iota(jnp.int32, (frames, N), 1)
    lane = lax.broadcasted_iota(jnp.int32, (frames, frames), 1)
    sub = lax.broadcasted_iota(jnp.int32, (frames, frames), 0)

    def to_columns(row):
        return jnp.transpose(jnp.broadcast_to(row, (frames, frames)))

    def is_label():
        label_col = to_columns(labels[...].astype(jnp.float32)).astype(jnp.int32)[:, 0:1]
        return (label_col - me * N) == lane_n

    steps = (V - 1) * NC
    stride = max(1, min((steps - 2) // nev, 2 * NC // CW))

    passed = (V - 2) * NC
    at_least = lambda i, a: jnp.minimum(jnp.maximum(i - a + 1, 0), 1)
    turn_left = (1 - at_least(v, 1)) * (1 - at_least(t, 1))
    turn_right = at_least(v, V - 1) * at_least(t, T - 1)

    def source(i, turn):
        j = i
        if M < NC:
            j = i + turn * ((NC - M) * at_least(i, M) - (passed + NC - M) * at_least(i, M + passed))
        return j // NC + 1, lax.rem(j, NC)

    def student_head():
        sw_copy.wait()
        each(1, T, lambda k: all_y(k, 1 - g).wait_recv())
        logits = jnp.dot(normed[...], wbuf[...], preferred_element_type=jnp.float32)
        label_logit = jnp.sum(jnp.where(is_label(), logits, 0.0), axis=1, keepdims=True)
        top = jnp.max(logits, axis=1, keepdims=True)
        total = jnp.sum(jnp.exp(logits - top), axis=1, keepdims=True)
        student_ref[...] = logits
        packed[...] = jnp.where(lane == 3, top, jnp.where(lane == 4, total, jnp.where(lane == 5, label_logit, 0.0)))

    student_at = steps - 4 if nev * stride < steps - 4 else None

    def step(i):
        @pl.when(i < steps)
        def _():
            k, c = source(i, turn_left)

            @pl.when(v + k < V)
            def _():
                take(v + k, c, go_left, v > 0)

            k, c = source(i, turn_right)

            @pl.when(v - k >= 0)
            def _():
                take(v - k, c, go_right, v < V - 1)

        if M < NC:
            @pl.when(i == passed - 1)
            def _():
                send_own(M, NC, late_left, late_right)

        j = i // stride - 1

        @pl.when((lax.rem(i, stride) == 0) & (j >= 0) & (j < nev))
        def _():
            pass_on(j)

        if spread_own:
            @pl.when((lax.rem(i, OWN) == OWN - 1) & (i // OWN < NC))
            def _():
                own_chunk(i // OWN)

        if student_at is not None:
            @pl.when(i == student_at)
            def _():
                student_head()

        @pl.when(i > 0)
        def _():
            k, c = source(i - 1, turn_left)

            @pl.when(v + k < V)
            def _():
                use(v + k, c)

            k, c = source(i - 1, turn_right)

            @pl.when(v - k >= 0)
            def _():
                use(v - k, c)

    each(0, steps + 1, step)
    each(min(nev, steps // stride), nev, pass_on)

    if student_at is None:
        student_head()
    student = student_ref[...]
    onehot = is_label()
    align_cols = to_columns(align[...].astype(jnp.float32)).astype(jnp.int32) - t * frames
    pick = (align_cols == lane).astype(jnp.bfloat16)

    def tin_wait(k):
        tt = lax.rem(t + k, T)
        remote(tin.at[tt], tin.at[tt], acc_send, acc_recv.at[tt], did(tt=tt)).wait_recv()

    each(1, T, tin_wait)
    for p in range(per):
        for h in range(H):
            total = acc[t * per + p, h]
            for k in range(1, T):
                total = total + tin[lax.rem(t + k, T), p, h]
            for ss in range(S):
                at = (p * S + ss) * rows + h * R
                bl[at:at + R, :] = total[ss * R:(ss + 1) * R]
    whole = bl[...]
    hi = whole.astype(jnp.bfloat16)
    rest = whole - hi.astype(jnp.float32)
    mid = rest.astype(jnp.bfloat16)
    low = (rest - mid.astype(jnp.float32)).astype(jnp.bfloat16)
    rows_of = lambda piece: jnp.dot(pick, piece, preferred_element_type=jnp.float32)
    aligned = (rows_of(low) + rows_of(mid)) + rows_of(hi)
    top_t = jnp.max(aligned, axis=1, keepdims=True)
    exp_t = jnp.exp(aligned - top_t)
    sum_t = jnp.sum(exp_t, axis=1, keepdims=True)
    cross_t = jnp.sum(exp_t * (aligned - student), axis=1, keepdims=True)

    pack = packed[...]
    for i, column in enumerate((top_t, sum_t, cross_t)):
        pack = jnp.where(lane == i, column, pack)
    stats[me] = jnp.transpose(pack)[0:8, :]

    def go_stat(k):
        where, other = vs_peer(k)
        return remote(stats.at[me], stats.at[me], stat_send, stat_recv, where)

    def farthest_first(k):
        high = at_least(v, V // 2)
        return high * k + (1 - high) * (VS - k)

    each(1, VS, lambda k: go_stat(farthest_first(k)).start())

    def peers(buf, send, recv):
        return remote(buf.at[0:VS - 1], buf.at[0:VS - 1], send, recv, did(ss=1 - s))

    peers(stats, stat_send, stat_recv).wait_recv()
    st = stats[...]
    row = lambda i: st[:, i, :]
    all_t = jnp.max(row(0), axis=0, keepdims=True)
    all_s = jnp.max(row(3), axis=0, keepdims=True)
    scale_t = jnp.exp(row(0) - all_t)
    scale_s = jnp.exp(row(3) - all_s)
    add = lambda x: jnp.sum(x, axis=0, keepdims=True)
    total_t = add(row(1) * scale_t)
    lse_t = all_t + jnp.log(total_t)
    lse_s = all_s + jnp.log(add(row(4) * scale_s))
    diverge = add(row(2) * scale_t) / total_t - lse_t + lse_s
    cross_term = lse_s - add(row(5))
    mask_float = mask[...].astype(jnp.float32)
    mask_count = jnp.sum(jnp.sum(mask_float, axis=1, keepdims=True), axis=0, keepdims=True)
    own_mask = mask[pl.ds(t, 1), :].astype(jnp.float32)
    row_weight = own_mask * (T * frames) / mask_count
    rl_out[...] = row_weight * (diverge + label_weight * cross_term)

    unpacked = jnp.where(sub == 0, lse_t, jnp.where(sub == 1, lse_s, row_weight))
    columns = jnp.transpose(unpacked)
    teacher_prob = jnp.exp(aligned - columns[:, 0:1])
    student_prob = jnp.exp(student - columns[:, 1:2])
    grad = (
        loss_scale * columns[:, 2:3]
        * ((1.0 + label_weight) * student_prob - teacher_prob - label_weight * onehot.astype(jnp.float32))
    ).astype(jnp.bfloat16)
    lg_out[...] = grad
    stores = [
        pltpu.make_async_copy(source, target, out_sem.at[i])
        for i, (source, target) in enumerate((
            (rl_out, rl_hbm),
            (lg_out, out_hbm.at[:, 0:N]),
            (hg_out, out_hbm.at[:, N:]),
        ))
    ]
    stores[0].start()
    stores[1].start()

    def go_inner(k):
        where, other = vs_peer(k)
        return remote(inner_in.at[me], inner_in.at[me], inner_send, inner_recv, where)

    def term(block):
        at = pl.multiple_of(block * w, w)
        return lax.dot_general(
            lg_out[...], wbuf[pl.ds(at, w), :], (((1,), (1,)), ((), ())), preferred_element_type=jnp.float32
        )

    def go_gs(b):
        return remote(sibout.at[b], sibin.at[b], gs_send, gs_recv.at[b], did(ss=1 - s))

    def order(q):
        return lax.rem(q, 2) * (q // 2) + (1 - lax.rem(q, 2)) * (V - 1 - q // 2)

    def for_sib(q):
        b = order(q)
        sibout[b] = term(b * S + 1 - s)
        go_gs(b).start()

    def for_own(q):
        b = order(q)
        part[b] = term(b * S + s)

    def piece(buf, b, p):
        return buf.at[b, pl.ds(pl.multiple_of(p * rp, rp), rp)]

    def go_line(buf, turn, b, p, onward):
        return remote(piece(part, b, p), piece(buf, b, p), ln_send, ln_recv.at[b + turn, p], did(vv=onward))

    def line(n, buf, turn, b_of, comes, onward):
        q, p = n // RP, lax.rem(n, RP)
        b = b_of(q)

        @pl.when(p == 0)
        def _():
            go_gs(b).wait_recv()
            part[b] += sibin[b]

        @pl.when(comes)
        def _():
            at = pl.ds(pl.multiple_of(p * rp, rp), rp)
            go_line(buf, turn, b, p, onward).wait_recv()
            part[b, at] += buf[b, at]

        go_line(buf, turn, b, p, onward).start()

    from_top, from_zero = (lambda q: V - 1 - q), (lambda q: q)

    def line_step(i):
        n = i - v * LAG

        @pl.when((n >= 0) & (n < (V - 1 - v) * RP))
        def _():
            line(n, rin, 1, from_top, v > 0, v + 1)

        m = i - (V - 1 - v) * LAG

        @pl.when((m >= 0) & (m < v * RP))
        def _():
            line(m, lin, 0, from_zero, v < V - 1, v - 1)

    each(0, 2, for_sib)
    each(0, 2, for_own)
    inner = jnp.sum(lg_out[...].astype(jnp.float32) * student_ref[...], axis=1, keepdims=True)
    inner_in[me] = jnp.transpose(jnp.broadcast_to(inner, (frames, frames)))[0:8, :]
    each(0, LAG, line_step)
    each(2, V, for_sib)
    each(2, V, for_own)
    each(1, VS, lambda k: go_inner(k).start())
    each(LAG, (V - 1) * max(RP, LAG), line_step)

    def sent(o):
        here = tbuf.at[:, o * S + s]

        @pl.when((o >= v) & (v > 0))
        def _():
            remote(here, here, left_send.at[o], z_recv.at[o, 0], did(vv=v - 1)).wait_send()

        @pl.when((o <= v) & (v < V - 1))
        def _():
            remote(here, here, right_send.at[o], z_recv.at[o, 0], did(vv=v + 1)).wait_send()


    each(0, V, sent)
    section = tbuf.at[:, 0:V]
    remote(section, section, sib_send, s_recv.at[0, 0], did(ss=1 - s)).wait_send()
    others = acc.at[0:V - per]
    remote(others, others, acc_send, acc_recv.at[t], did(ss=1 - s)).wait_send()

    def w_sent(k):
        all_x(k).wait_send()
        all_y(k, g).wait_send()

    each(1, T, w_sent)
    remote(sibout, sibout, gs_send, gs_recv.at[0], did(ss=1 - s)).wait_send()
    peers(stats, stat_send, stat_recv).wait_send()
    peers(inner_in, inner_send, inner_recv).wait_send()
    peers(inner_in, inner_send, inner_recv).wait_recv()
    inner_total = jnp.sum(inner_in[...], axis=0)[0:1, :]
    inner_rows = to_columns(inner_total)[:, 0:1]

    go_gs(v).wait_recv()
    part[v] += sibin[v]

    def last(buf, turn, onward):
        each(0, RP, lambda p: go_line(buf, turn, v, p, onward).wait_recv())
        part[v] += buf[v]

    @pl.when(v > 0)
    def _():
        last(rin, 1, v - 1)

    @pl.when(v < V - 1)
    def _():
        last(lin, 0, v + 1)

    mine = pl.multiple_of(me * w, w)
    scaled = part[v] * gain[:, pl.ds(mine, w)]
    own_hidden = sh[:, pl.ds(mine, w)].astype(jnp.float32)
    hg_out[...] = (inverse * scaled - own_hidden * (inverse**2 * inner_rows / DS)).astype(jnp.bfloat16)

    stores[2].start()

    some = part.at[0:V - 1]
    remote(some, some, ln_send, ln_recv.at[0, 0], did(ss=1 - s)).wait_send()
    for store in stores:
        store.wait()


def spread(loss_in, both_in, loss_hbm, grad_hbm, hidden_hbm, loss, grad, hidden, sem):
    N = grad.shape[1]
    loads = [
        pltpu.make_async_copy(source, target, sem.at[i])
        for i, (source, target) in enumerate(
            ((both_in.at[:, 0:N], grad), (both_in.at[:, N:], hidden), (loss_in, loss))
        )
    ]
    stores = [
        pltpu.make_async_copy(source, target, sem.at[i])
        for i, (source, target) in enumerate(((grad, grad_hbm), (hidden, hidden_hbm), (loss, loss_hbm)))
    ]
    for load in loads:
        load.start()
    for load, store in zip(loads, stores):
        load.wait()
        store.start()
    for store in stores:
        store.wait()


def local(sizes, teacher_hidden, teacher_weight, student_hidden, student_gain, student_weight, labels, alignment, loss_mask):
    G, V, T, S, H, C, CW, RP, LAG, M, OWN = sizes
    VS = V * S
    NC = H * C
    rows, width = teacher_hidden.shape
    R = rows // H
    fc = width // C
    N = teacher_weight.shape[1]
    frames, DS = student_hidden.shape
    w = DS // VS
    per = V // T
    f32, bf16 = jnp.float32, jnp.bfloat16
    dma = pltpu.SemaphoreType.DMA
    hbm = pl.BlockSpec(memory_space=pl.ANY)
    row_loss, both = pl.pallas_call(
        functools.partial(kernel, sizes),
        out_shape=(jax.ShapeDtypeStruct((1, frames), f32), jax.ShapeDtypeStruct((frames, N + w), bf16)),
        in_specs=[hbm] * 8,
        out_specs=(hbm, hbm),
        scratch_shapes=[
            pltpu.VMEM((frames, DS), bf16),
            pltpu.VMEM((1, DS), f32),
            pltpu.VMEM((1, frames), jnp.int32),
            pltpu.VMEM((1, frames), jnp.int32),
            pltpu.VMEM((T, frames), jnp.int32),
            pltpu.VMEM((1, frames), f32),
            pltpu.VMEM((frames, N), bf16),
            pltpu.VMEM((frames, w), bf16),
            pltpu.VMEM((NC, VS, R, fc), bf16),
            pltpu.VMEM((C, fc, N), bf16),
            pltpu.VMEM((DS, N), bf16),
            pltpu.VMEM((frames, DS), bf16),
            pltpu.VMEM((V, H, S * R, N), f32),
            pltpu.VMEM((T, per, H, S * R, N), f32),
            pltpu.VMEM((frames, N), f32),
            pltpu.VMEM((VS, 8, frames), f32),
            pltpu.VMEM((VS, 8, frames), f32),
            pltpu.VMEM((V, frames, w), f32),
            pltpu.VMEM((V, frames, w), f32),
            pltpu.VMEM((V, frames, w), f32),
            pltpu.VMEM((V, frames, w), f32),
            pltpu.VMEM((V, frames, w), f32),
            pltpu.VMEM((frames, N), f32),
            pltpu.VMEM((frames, frames), f32),
            dma, dma, dma, dma((5,)), dma((3,)),
            dma((V,)), dma((V,)), dma, dma((V, NC)), dma((V, NC)),
            dma((T,)), dma((T - 1, CW)), dma((T,)), dma((T,)),
            dma, dma((T,)),
            dma, dma, dma, dma,
            dma, dma((V,)), dma, dma((V + 1, RP)),
        ],
        compiler_params=pltpu.CompilerParams(
            collective_id=0, has_side_effects=True, vmem_limit_bytes=63 * 2**20
        ),
    )(
        teacher_hidden, teacher_weight, student_hidden, student_gain.reshape(1, DS), student_weight,
        labels.reshape(1, frames), alignment.reshape(1, frames), loss_mask.reshape(T, frames),
    )
    row_loss, logit_grad, hidden_grad = pl.pallas_call(
        spread,
        out_shape=(
            jax.ShapeDtypeStruct((1, frames), f32),
            jax.ShapeDtypeStruct((frames, N), bf16),
            jax.ShapeDtypeStruct((frames, w), bf16),
        ),
        in_specs=[hbm] * 2,
        out_specs=(hbm,) * 3,
        scratch_shapes=[pltpu.VMEM((1, frames), f32), pltpu.VMEM((frames, N), bf16), pltpu.VMEM((frames, w), bf16), dma((3,))],
    )(row_loss, both)
    return row_loss.reshape(frames), logit_grad, hidden_grad


def solution(mesh):
    sizes = tuple(mesh.shape[a] for a in ("groups", "vocab", "tokens", "section")) + (2, 4, 8, 4, 2, 4, 2)
    in_specs = (
        P(("groups", "vocab", "section"), "tokens"),
        P("tokens", ("vocab", "section")),
        P(("groups", "tokens"), None),
        P(),
        P("tokens", ("vocab", "section")),
        P(("groups", "tokens")),
        P(("groups", "tokens")),
        P("groups"),
    )
    out_specs = (
        P(("groups", "tokens")),
        P(("groups", "tokens"), ("vocab", "section")),
        P(("groups", "tokens"), ("vocab", "section")),
    )
    return jax.shard_map(
        functools.partial(local, sizes), mesh=mesh, in_specs=in_specs, out_specs=out_specs, check_vma=False
    )
```

```python
import functools

import jax
import jax.numpy as jnp
from jax import lax
from jax.experimental import pallas as pl
from jax.experimental.pallas import tpu as pltpu
from jax.sharding import PartitionSpec as P

label_weight = 0.2
loss_scale = 16.0
epsilon = 1e-05
MESH = pl.DeviceIdType.MESH


def kernel(
    sizes, th, tw, sh_in, gain_in, sw, labels_in, align_in, mask_in,
    rl_hbm, out_hbm,
    sh, gain, labels, align, mask, rl_out, lg_out, hg_out,
    tbuf, twv, wbuf, normed, acc, tin, bl, stats, inner_in, sibout, sibin, part, rin, lin, student_ref, packed, turned, pick_ref,
    tw_sem, own_sem, sw_sem, in_sem, out_sem,
    left_send, right_send, sib_send, z_recv, s_recv,
    x_send, x_recv, y_send, y_recv,
    acc_send, acc_recv,
    stat_send, stat_recv, inner_send, inner_recv,
    gs_send, gs_recv, ln_send, ln_recv,
):
    G, V, T, S, H, C, CW, RP, LAG, M, OWN = sizes
    NC = H * C
    VS = V * S
    M = M if T == 2 and V > 2 else NC
    g, v, t, s = (lax.axis_index(a) for a in ("groups", "vocab", "tokens", "section"))
    me = v * S + s
    rows = th.shape[0]
    R = rows // H
    fc = th.shape[1] // C
    F = sw.shape[0]
    half = F // 2
    wc = half // CW
    frames, DS = sh.shape
    N = tw.shape[1]
    w = DS // VS
    per = V // T
    rp = frames // RP

    def did(gg=None, vv=None, tt=None, ss=None):
        pick = lambda a, b: b if a is None else a
        return (pick(gg, g), pick(vv, v), pick(tt, t), pick(ss, s))

    def remote(src, dst, send, recv, where):
        return pltpu.make_async_remote_copy(
            src_ref=src, dst_ref=dst, send_sem=send, recv_sem=recv,
            device_id=where, device_id_type=MESH,
        )

    def vs_peer(k):
        other = lax.rem(me + k, VS)
        return did(vv=other // S, ss=lax.rem(other, S)), other

    def each(lo, hi, body):
        def run(i, carry):
            body(i)
            return carry
        lax.fori_loop(lo, hi, run, 0)

    barrier = pltpu.get_barrier_semaphore()

    def greet(where):
        pl.semaphore_signal(barrier, inc=1, device_id=where, device_id_type=MESH)

    loads = [
        pltpu.make_async_copy(source, target, in_sem.at[i])
        for i, (source, target) in enumerate(
            ((sh_in, sh), (gain_in, gain), (labels_in, labels), (align_in, align), (mask_in, mask))
        )
    ]
    for load in loads:
        load.start()
    def th_at(cc):
        h, c = cc // C, cc % C
        return th.at[h * R:(h + 1) * R, c * fc:(c + 1) * fc]

    for c in range(C):
        pltpu.make_async_copy(tw.at[c * fc:(c + 1) * fc], twv.at[c], tw_sem).start()
    for cc in range(NC):
        pltpu.make_async_copy(th_at(cc), tbuf.at[cc, me], own_sem).start()
    sw_copy = pltpu.make_async_copy(sw, wbuf.at[pl.ds(pl.multiple_of(t * F, F), F)], sw_sem)
    sw_copy.start()

    each(1, VS, lambda k: greet(vs_peer(k)[0]))
    each(1, T, lambda k: greet(did(tt=lax.rem(t + k, T))))
    greet(did(gg=1 - g))
    pl.semaphore_wait(barrier, VS - 1 + T - 1 + 1)

    def go_left(o, c, src):
        return remote(src, tbuf.at[c, o * S + s], left_send.at[o], z_recv.at[o, c], did(vv=v - 1))

    def go_right(o, c, src):
        return remote(src, tbuf.at[c, o * S + s], right_send.at[o], z_recv.at[o, c], did(vv=v + 1))

    def go_sib(o, c, src):
        return remote(src, tbuf.at[c, o * S + s], sib_send, s_recv.at[o, c], did(ss=1 - s))

    late_left = (v == 1) & (t == 0)
    late_right = (v == V - 2) & (t == T - 1)

    def send_own(lo, hi, to_left, to_right):
        for cc in range(lo, hi):
            @pl.when(to_left)
            def _():
                go_left(v, cc, th_at(cc)).start()

            @pl.when(to_right)
            def _():
                go_right(v, cc, th_at(cc)).start()

    send_own(0, M, v > 0, v < V - 1)
    send_own(M, NC, (v > 0) & jnp.logical_not(late_left), (v < V - 1) & jnp.logical_not(late_right))

    def w_at(tt, hh, cw):
        return wbuf.at[pl.ds(pl.multiple_of(tt * F + hh * half + cw * wc, wc), wc)]

    def go_x(k, cw):
        to = lax.rem(t + k, T)
        src = sw.at[pl.ds(pl.multiple_of(g * half + cw * wc, wc), wc)]
        return remote(src, w_at(t, g, cw), x_send.at[to], x_recv.at[k - 1, cw], did(tt=to))

    def go_y(tt, cw):
        return remote(w_at(tt, g, cw), w_at(tt, g, cw), y_send.at[tt], y_recv.at[tt], did(gg=1 - g))

    def x_wait(k, tt, cw):
        remote(w_at(tt, g, cw), w_at(tt, g, cw), x_send.at[tt], x_recv.at[k - 1, cw], did(tt=tt)).wait_recv()

    def w_half(tt, hh):
        return wbuf.at[pl.ds(pl.multiple_of(tt * F + hh * half, half), half)]

    def all_x(k):
        to = lax.rem(t + k, T)
        return remote(w_half(t, g), w_half(t, g), x_send.at[to], x_recv.at[0, 0], did(tt=to))

    def all_y(k, hh):
        tt = lax.rem(t + k, T)
        return remote(w_half(tt, hh), w_half(tt, hh), y_send.at[tt], y_recv.at[tt], did(gg=1 - g))

    nev = (T - 1) * CW
    each(0, nev, lambda j: go_x(j // CW + 1, lax.rem(j, CW)).start())
    for cc in range(NC):
        go_sib(v, cc, th_at(cc)).start()

    def pass_on(j):
        tt = lax.rem(t + T - 1 - j // CW, T)
        cw = lax.rem(j, CW)
        x_wait(j // CW + 1, tt, cw)
        go_y(tt, cw).start()

    for load in loads:
        load.wait()
    hid = sh[...].astype(jnp.float32)
    inverse = lax.rsqrt(jnp.mean(hid * hid, axis=1, keepdims=True) + epsilon)
    normed[...] = (hid * inverse * gain[...]).astype(jnp.bfloat16)

    def multiply(o, cc):
        x = tbuf[cc, pl.ds(o * S, S)].reshape(S * R, fc)
        acc[o, cc // C] += jnp.dot(x, twv[lax.rem(cc, C)], preferred_element_type=jnp.float32)

    def go_acc(o, h):
        p = lax.rem(o, per)
        return remote(acc.at[o, h], tin.at[t, p, h], acc_send, acc_recv.at[t], did(tt=o // per))

    def finished(o, cc):
        @pl.when((lax.rem(cc, C) == C - 1) & (o // per != t))
        def _():
            go_acc(o, cc // C).start()

    acc[...] = jnp.zeros_like(acc)

    pltpu.make_async_copy(tbuf.at[:, me], tbuf.at[:, me], own_sem).wait()
    pltpu.make_async_copy(twv, twv, tw_sem).wait()

    def own_chunk(c):
        other = tbuf.at[c, v * S + 1 - s]
        remote(other, other, sib_send, s_recv.at[v, c], did(ss=1 - s)).wait_recv()
        multiply(v, c)
        finished(v, c)

    spread_own = V > 2
    if not spread_own:
        each(0, NC, own_chunk)

    def take(o, c, onward, has_next):
        here = tbuf.at[c, o * S + s]
        remote(here, here, sib_send, z_recv.at[o, c], did(ss=1 - s)).wait_recv()

        @pl.when(has_next)
        def _():
            onward(o, c, here).start()

        go_sib(o, c, here).start()

    def use(o, c):
        other = tbuf.at[c, o * S + 1 - s]
        remote(other, other, sib_send, s_recv.at[o, c], did(ss=1 - s)).wait_recv()
        multiply(o, c)
        finished(o, c)

    lane_n = lax.broadcasted_iota(jnp.int32, (frames, N), 1)
    lane = lax.broadcasted_iota(jnp.int32, (frames, frames), 1)
    sub = lax.broadcasted_iota(jnp.int32, (frames, frames), 0)

    def to_columns(row):
        return jnp.transpose(jnp.broadcast_to(row, (frames, frames)))

    def is_label():
        label_col = to_columns(labels[...].astype(jnp.float32)).astype(jnp.int32)[:, 0:1]
        return (label_col - me * N) == lane_n

    steps = (V - 1) * NC
    stride = max(1, min((steps - 2) // nev, 2 * NC // CW))

    passed = (V - 2) * NC
    at_least = lambda i, a: jnp.minimum(jnp.maximum(i - a + 1, 0), 1)
    turn_left = (1 - at_least(v, 1)) * (1 - at_least(t, 1))
    turn_right = at_least(v, V - 1) * at_least(t, T - 1)

    def source(i, turn):
        j = i
        if M < NC:
            j = i + turn * ((NC - M) * at_least(i, M) - (passed + NC - M) * at_least(i, M + passed))
        return j // NC + 1, lax.rem(j, NC)

    def student_head():
        sw_copy.wait()
        each(1, T, lambda k: all_y(k, 1 - g).wait_recv())
        logits = jnp.dot(normed[...], wbuf[...], preferred_element_type=jnp.float32)
        label_logit = jnp.sum(jnp.where(is_label(), logits, 0.0), axis=1, keepdims=True)
        top = jnp.max(logits, axis=1, keepdims=True)
        total = jnp.sum(jnp.exp(logits - top), axis=1, keepdims=True)
        student_ref[...] = logits
        align_cols = to_columns(align[...].astype(jnp.float32)).astype(jnp.int32) - t * frames
        pick_ref[...] = (align_cols == lane).astype(jnp.bfloat16)
        packed[...] = jnp.where(lane == 3, top, jnp.where(lane == 4, total, jnp.where(lane == 5, label_logit, 0.0)))

    student_at = steps - 4 if nev * stride < steps - 4 else None

    def step(i):
        @pl.when(i < steps)
        def _():
            k, c = source(i, turn_left)

            @pl.when(v + k < V)
            def _():
                take(v + k, c, go_left, v > 0)

            k, c = source(i, turn_right)

            @pl.when(v - k >= 0)
            def _():
                take(v - k, c, go_right, v < V - 1)

        if M < NC:
            @pl.when(i == passed - 1)
            def _():
                send_own(M, NC, late_left, late_right)

        j = i // stride - 1

        @pl.when((lax.rem(i, stride) == 0) & (j >= 0) & (j < nev))
        def _():
            pass_on(j)

        if spread_own:
            @pl.when((lax.rem(i, OWN) == OWN - 1) & (i // OWN < NC))
            def _():
                own_chunk(i // OWN)

        if student_at is not None:
            @pl.when(i == student_at)
            def _():
                student_head()

        @pl.when(i > 0)
        def _():
            k, c = source(i - 1, turn_left)

            @pl.when(v + k < V)
            def _():
                use(v + k, c)

            k, c = source(i - 1, turn_right)

            @pl.when(v - k >= 0)
            def _():
                use(v - k, c)

    each(0, steps + 1, step)
    each(min(nev, steps // stride), nev, pass_on)

    if student_at is None:
        student_head()
    student = student_ref[...]
    onehot = is_label()
    def tin_wait(k):
        tt = lax.rem(t + k, T)
        remote(tin.at[tt], tin.at[tt], acc_send, acc_recv.at[tt], did(tt=tt)).wait_recv()

    each(1, T, tin_wait)
    for p in range(per):
        for h in range(H):
            total = acc[t * per + p, h]
            for k in range(1, T):
                total = total + tin[lax.rem(t + k, T), p, h]
            for ss in range(S):
                at = (p * S + ss) * rows + h * R
                bl[at:at + R, :] = total[ss * R:(ss + 1) * R]
    whole = bl[...]
    hi = whole.astype(jnp.bfloat16)
    rest = whole - hi.astype(jnp.float32)
    mid = rest.astype(jnp.bfloat16)
    low = (rest - mid.astype(jnp.float32)).astype(jnp.bfloat16)
    rows_of = lambda piece: jnp.dot(pick_ref[...], piece, preferred_element_type=jnp.float32)
    aligned = (rows_of(low) + rows_of(mid)) + rows_of(hi)
    top_t = jnp.max(aligned, axis=1, keepdims=True)
    exp_t = jnp.exp(aligned - top_t)
    sum_t = jnp.sum(exp_t, axis=1, keepdims=True)
    cross_t = jnp.sum(exp_t * (aligned - student), axis=1, keepdims=True)

    pack = packed[...]
    for i, column in enumerate((top_t, sum_t, cross_t)):
        pack = jnp.where(lane == i, column, pack)
    stats[me] = jnp.transpose(pack)[0:8, :]

    def go_stat(k):
        where, other = vs_peer(k)
        return remote(stats.at[me], stats.at[me], stat_send, stat_recv, where)

    def farthest_first(k):
        high = at_least(v, V // 2)
        return high * k + (1 - high) * (VS - k)

    each(1, VS, lambda k: go_stat(farthest_first(k)).start())

    def peers(buf, send, recv):
        return remote(buf.at[0:VS - 1], buf.at[0:VS - 1], send, recv, did(ss=1 - s))

    def turn_block(b):
        turned[b] = jnp.transpose(wbuf[pl.ds(pl.multiple_of(b * w, w), w), :])

    each(0, VS, turn_block)
    peers(stats, stat_send, stat_recv).wait_recv()
    st = stats[...]
    row = lambda i: st[:, i, :]
    all_t = jnp.max(row(0), axis=0, keepdims=True)
    all_s = jnp.max(row(3), axis=0, keepdims=True)
    scale_t = jnp.exp(row(0) - all_t)
    scale_s = jnp.exp(row(3) - all_s)
    add = lambda x: jnp.sum(x, axis=0, keepdims=True)
    total_t = add(row(1) * scale_t)
    lse_t = all_t + jnp.log(total_t)
    lse_s = all_s + jnp.log(add(row(4) * scale_s))
    diverge = add(row(2) * scale_t) / total_t - lse_t + lse_s
    cross_term = lse_s - add(row(5))
    mask_float = mask[...].astype(jnp.float32)
    mask_count = jnp.sum(jnp.sum(mask_float, axis=1, keepdims=True), axis=0, keepdims=True)
    own_mask = mask[pl.ds(t, 1), :].astype(jnp.float32)
    row_weight = own_mask * (T * frames) / mask_count
    rl_out[...] = row_weight * (diverge + label_weight * cross_term)

    unpacked = jnp.where(sub == 0, lse_t, jnp.where(sub == 1, lse_s, row_weight))
    columns = jnp.transpose(unpacked)
    teacher_prob = jnp.exp(aligned - columns[:, 0:1])
    student_prob = jnp.exp(student - columns[:, 1:2])
    grad = (
        loss_scale * columns[:, 2:3]
        * ((1.0 + label_weight) * student_prob - teacher_prob - label_weight * onehot.astype(jnp.float32))
    ).astype(jnp.bfloat16)
    lg_out[...] = grad
    stores = [
        pltpu.make_async_copy(source, target, out_sem.at[i])
        for i, (source, target) in enumerate((
            (rl_out, rl_hbm),
            (lg_out, out_hbm.at[:, 0:N]),
            (hg_out, out_hbm.at[:, N:]),
        ))
    ]
    stores[0].start()
    stores[1].start()

    def go_inner(k):
        where, other = vs_peer(k)
        return remote(inner_in.at[me], inner_in.at[me], inner_send, inner_recv, where)

    def term(block):
        return jnp.dot(lg_out[...], turned[block], preferred_element_type=jnp.float32)

    def piece(buf, b, p):
        return buf.at[b, pl.ds(pl.multiple_of(p * rp, rp), rp)]

    def go_gs(b, p):
        return remote(piece(sibout, b, p), piece(sibin, b, p), gs_send, gs_recv.at[b, p], did(ss=1 - s))

    def order(q):
        b = lax.rem(q, 2) * (q // 2) + (1 - lax.rem(q, 2)) * (V - 1 - q // 2)
        high = at_least(v, V // 2)
        return high * (V - 1 - b) + (1 - high) * b

    def first_sib(p):
        b = order(0)
        at = pl.ds(pl.multiple_of(p * rp, rp), rp)
        sibout[b, at] = jnp.dot(lg_out[at, :], turned[b * S + 1 - s], preferred_element_type=jnp.float32)
        go_gs(b, p).start()

    def for_sib(q):
        b = order(q)
        sibout[b] = term(b * S + 1 - s)
        each(0, RP, lambda p: go_gs(b, p).start())

    def for_own(q):
        b = order(q)
        part[b] = term(b * S + s)

    def go_line(buf, turn, b, p, onward):
        return remote(piece(part, b, p), piece(buf, b, p), ln_send, ln_recv.at[b + turn, p], did(vv=onward))

    def line(n, buf, turn, b_of, comes, onward):
        q, p = n // RP, lax.rem(n, RP)
        b = b_of(q)

        at = pl.ds(pl.multiple_of(p * rp, rp), rp)
        go_gs(b, p).wait_recv()
        part[b, at] += sibin[b, at]

        @pl.when(comes)
        def _():
            go_line(buf, turn, b, p, onward).wait_recv()
            part[b, at] += buf[b, at]

        go_line(buf, turn, b, p, onward).start()

    from_top, from_zero = (lambda q: V - 1 - q), (lambda q: q)

    def line_step(i):
        n = i - v * LAG

        @pl.when((n >= 0) & (n < (V - 1 - v) * RP))
        def _():
            line(n, rin, 1, from_top, v > 0, v + 1)

        m = i - (V - 1 - v) * LAG

        @pl.when((m >= 0) & (m < v * RP))
        def _():
            line(m, lin, 0, from_zero, v < V - 1, v - 1)

    each(0, RP, first_sib)
    for_own(0)
    for_sib(1)
    inner = jnp.sum(lg_out[...].astype(jnp.float32) * student_ref[...], axis=1, keepdims=True)
    inner_in[me] = jnp.transpose(jnp.broadcast_to(inner, (frames, frames)))[0:8, :]
    each(0, LAG, line_step)
    for_own(1)
    each(2, V, for_sib)
    each(2, V, for_own)
    each(1, VS, lambda k: go_inner(k).start())
    each(LAG, (V - 1) * max(RP, LAG), line_step)

    def sent(o):
        here = tbuf.at[:, o * S + s]

        @pl.when((o >= v) & (v > 0))
        def _():
            remote(here, here, left_send.at[o], z_recv.at[o, 0], did(vv=v - 1)).wait_send()

        @pl.when((o <= v) & (v < V - 1))
        def _():
            remote(here, here, right_send.at[o], z_recv.at[o, 0], did(vv=v + 1)).wait_send()


    each(0, V, sent)
    section = tbuf.at[:, 0:V]
    remote(section, section, sib_send, s_recv.at[0, 0], did(ss=1 - s)).wait_send()
    others = acc.at[0:V - per]
    remote(others, others, acc_send, acc_recv.at[t], did(ss=1 - s)).wait_send()

    def w_sent(k):
        all_x(k).wait_send()
        all_y(k, g).wait_send()

    each(1, T, w_sent)
    remote(sibout, sibout, gs_send, gs_recv.at[0, 0], did(ss=1 - s)).wait_send()
    peers(stats, stat_send, stat_recv).wait_send()
    peers(inner_in, inner_send, inner_recv).wait_send()
    peers(inner_in, inner_send, inner_recv).wait_recv()
    inner_total = jnp.sum(inner_in[...], axis=0)[0:1, :]
    inner_rows = to_columns(inner_total)[:, 0:1]

    each(0, RP, lambda p: go_gs(v, p).wait_recv())
    part[v] += sibin[v]

    def last(buf, turn, onward):
        each(0, RP, lambda p: go_line(buf, turn, v, p, onward).wait_recv())
        part[v] += buf[v]

    @pl.when(v > 0)
    def _():
        last(rin, 1, v - 1)

    @pl.when(v < V - 1)
    def _():
        last(lin, 0, v + 1)

    mine = pl.multiple_of(me * w, w)
    scaled = part[v] * gain[:, pl.ds(mine, w)]
    own_hidden = sh[:, pl.ds(mine, w)].astype(jnp.float32)
    hg_out[...] = (inverse * scaled - own_hidden * (inverse**2 * inner_rows / DS)).astype(jnp.bfloat16)

    stores[2].start()

    some = part.at[0:V - 1]
    remote(some, some, ln_send, ln_recv.at[0, 0], did(ss=1 - s)).wait_send()
    for store in stores:
        store.wait()


def spread(loss_in, both_in, loss_hbm, grad_hbm, hidden_hbm, loss, grad, hidden, sem):
    N = grad.shape[1]
    loads = [
        pltpu.make_async_copy(source, target, sem.at[i])
        for i, (source, target) in enumerate(
            ((both_in.at[:, 0:N], grad), (both_in.at[:, N:], hidden), (loss_in, loss))
        )
    ]
    stores = [
        pltpu.make_async_copy(source, target, sem.at[i])
        for i, (source, target) in enumerate(((grad, grad_hbm), (hidden, hidden_hbm), (loss, loss_hbm)))
    ]
    for load in loads:
        load.start()
    for load, store in zip(loads, stores):
        load.wait()
        store.start()
    for store in stores:
        store.wait()


def local(sizes, teacher_hidden, teacher_weight, student_hidden, student_gain, student_weight, labels, alignment, loss_mask):
    G, V, T, S, H, C, CW, RP, LAG, M, OWN = sizes
    VS = V * S
    NC = H * C
    rows, width = teacher_hidden.shape
    R = rows // H
    fc = width // C
    N = teacher_weight.shape[1]
    frames, DS = student_hidden.shape
    w = DS // VS
    per = V // T
    f32, bf16 = jnp.float32, jnp.bfloat16
    dma = pltpu.SemaphoreType.DMA
    hbm = pl.BlockSpec(memory_space=pl.ANY)
    row_loss, both = pl.pallas_call(
        functools.partial(kernel, sizes),
        out_shape=(jax.ShapeDtypeStruct((1, frames), f32), jax.ShapeDtypeStruct((frames, N + w), bf16)),
        in_specs=[hbm] * 8,
        out_specs=(hbm, hbm),
        scratch_shapes=[
            pltpu.VMEM((frames, DS), bf16),
            pltpu.VMEM((1, DS), f32),
            pltpu.VMEM((1, frames), jnp.int32),
            pltpu.VMEM((1, frames), jnp.int32),
            pltpu.VMEM((T, frames), jnp.int32),
            pltpu.VMEM((1, frames), f32),
            pltpu.VMEM((frames, N), bf16),
            pltpu.VMEM((frames, w), bf16),
            pltpu.VMEM((NC, VS, R, fc), bf16),
            pltpu.VMEM((C, fc, N), bf16),
            pltpu.VMEM((DS, N), bf16),
            pltpu.VMEM((frames, DS), bf16),
            pltpu.VMEM((V, H, S * R, N), f32),
            pltpu.VMEM((T, per, H, S * R, N), f32),
            pltpu.VMEM((frames, N), f32),
            pltpu.VMEM((VS, 8, frames), f32),
            pltpu.VMEM((VS, 8, frames), f32),
            pltpu.VMEM((V, frames, w), f32),
            pltpu.VMEM((V, frames, w), f32),
            pltpu.VMEM((V, frames, w), f32),
            pltpu.VMEM((V, frames, w), f32),
            pltpu.VMEM((V, frames, w), f32),
            pltpu.VMEM((frames, N), f32),
            pltpu.VMEM((frames, frames), f32),
            pltpu.VMEM((VS, N, w), bf16),
            pltpu.VMEM((frames, frames), bf16),
            dma, dma, dma, dma((5,)), dma((3,)),
            dma((V,)), dma((V,)), dma, dma((V, NC)), dma((V, NC)),
            dma((T,)), dma((T - 1, CW)), dma((T,)), dma((T,)),
            dma, dma((T,)),
            dma, dma, dma, dma,
            dma, dma((V, RP)), dma, dma((V + 1, RP)),
        ],
        compiler_params=pltpu.CompilerParams(
            collective_id=0, has_side_effects=True, vmem_limit_bytes=63 * 2**20
        ),
    )(
        teacher_hidden, teacher_weight, student_hidden, student_gain.reshape(1, DS), student_weight,
        labels.reshape(1, frames), alignment.reshape(1, frames), loss_mask.reshape(T, frames),
    )
    row_loss, logit_grad, hidden_grad = pl.pallas_call(
        spread,
        out_shape=(
            jax.ShapeDtypeStruct((1, frames), f32),
            jax.ShapeDtypeStruct((frames, N), bf16),
            jax.ShapeDtypeStruct((frames, w), bf16),
        ),
        in_specs=[hbm] * 2,
        out_specs=(hbm,) * 3,
        scratch_shapes=[pltpu.VMEM((1, frames), f32), pltpu.VMEM((frames, N), bf16), pltpu.VMEM((frames, w), bf16), dma((3,))],
    )(row_loss, both)
    return row_loss.reshape(frames), logit_grad, hidden_grad


def solution(mesh):
    sizes = tuple(mesh.shape[a] for a in ("groups", "vocab", "tokens", "section")) + (2, 4, 8, 4, 2, 4, 2)
    in_specs = (
        P(("groups", "vocab", "section"), "tokens"),
        P("tokens", ("vocab", "section")),
        P(("groups", "tokens"), None),
        P(),
        P("tokens", ("vocab", "section")),
        P(("groups", "tokens")),
        P(("groups", "tokens")),
        P("groups"),
    )
    out_specs = (
        P(("groups", "tokens")),
        P(("groups", "tokens"), ("vocab", "section")),
        P(("groups", "tokens"), ("vocab", "section")),
    )
    return jax.shard_map(
        functools.partial(local, sizes), mesh=mesh, in_specs=in_specs, out_specs=out_specs, check_vma=False
    )
```

```python
import functools

import jax
import jax.numpy as jnp
from jax import lax
from jax.experimental import pallas as pl
from jax.experimental.pallas import tpu as pltpu
from jax.sharding import PartitionSpec as P

label_weight = 0.2
loss_scale = 16.0
epsilon = 1e-05
MESH = pl.DeviceIdType.MESH


def kernel(
    sizes, th, tw, sh_in, gain_in, sw, labels_in, align_in, mask_in,
    rl_hbm, out_hbm,
    sh, gain, labels, align, mask, rl_out, lg_out, hg_out,
    tbuf, twv, wbuf, normed, acc, tin, bl, stats, inner_in, sibout, sibin, part, rin, lin, student_ref, packed, turned, pick_ref,
    tw_sem, own_sem, sw_sem, in_sem, out_sem,
    z_send, sib_send, z_recv, s_recv,
    x_send, x_recv, y_send, y_recv,
    acc_send, acc_recv,
    stat_send, stat_recv, inner_send, inner_recv,
    gs_send, gs_recv, ln_send, ln_recv,
):
    G, V, T, S, H, C, CW, RP, LAG, M, OWN = sizes
    NC = H * C
    VS = V * S
    M = M if T == 2 and V > 2 else NC
    g, v, t, s = (lax.axis_index(a) for a in ("groups", "vocab", "tokens", "section"))
    me = v * S + s
    rows = th.shape[0]
    R = rows // H
    fc = th.shape[1] // C
    F = sw.shape[0]
    half = F // 2
    wc = half // CW
    frames, DS = sh.shape
    N = tw.shape[1]
    w = DS // VS
    per = V // T
    rp = frames // RP

    def did(gg=None, vv=None, tt=None, ss=None):
        pick = lambda a, b: b if a is None else a
        return (pick(gg, g), pick(vv, v), pick(tt, t), pick(ss, s))

    def remote(src, dst, send, recv, where):
        return pltpu.make_async_remote_copy(
            src_ref=src, dst_ref=dst, send_sem=send, recv_sem=recv,
            device_id=where, device_id_type=MESH,
        )

    def vs_peer(k):
        other = lax.rem(me + k, VS)
        return did(vv=other // S, ss=lax.rem(other, S)), other

    def each(lo, hi, body):
        def run(i, carry):
            body(i)
            return carry
        lax.fori_loop(lo, hi, run, 0)

    barrier = pltpu.get_barrier_semaphore()

    def greet(where):
        pl.semaphore_signal(barrier, inc=1, device_id=where, device_id_type=MESH)

    loads = [
        pltpu.make_async_copy(source, target, in_sem.at[i])
        for i, (source, target) in enumerate(
            ((sh_in, sh), (gain_in, gain), (labels_in, labels), (align_in, align), (mask_in, mask))
        )
    ]
    for load in loads:
        load.start()
    def th_at(cc):
        h, c = cc // C, cc % C
        return th.at[h * R:(h + 1) * R, c * fc:(c + 1) * fc]

    for c in range(C):
        pltpu.make_async_copy(tw.at[c * fc:(c + 1) * fc], twv.at[c], tw_sem).start()
    for cc in range(NC):
        pltpu.make_async_copy(th_at(cc), tbuf.at[cc, me], own_sem).start()
    sw_copy = pltpu.make_async_copy(sw, wbuf.at[pl.ds(pl.multiple_of(t * F, F), F)], sw_sem)
    sw_copy.start()

    each(1, VS, lambda k: greet(vs_peer(k)[0]))
    each(1, T, lambda k: greet(did(tt=lax.rem(t + k, T))))
    greet(did(gg=1 - g))
    pl.semaphore_wait(barrier, VS - 1 + T - 1 + 1)

    def go_left(o, c, src):
        return remote(src, tbuf.at[c, o * S + s], z_send, z_recv.at[o - 1, c], did(vv=v - 1))

    def go_right(o, c, src):
        return remote(src, tbuf.at[c, o * S + s], z_send, z_recv.at[o, c], did(vv=v + 1))

    def go_sib(o, c, src):
        return remote(src, tbuf.at[c, o * S + s], sib_send, s_recv.at[o, c], did(ss=1 - s))

    late_left = (v == 1) & (t == 0)
    late_right = (v == V - 2) & (t == T - 1)

    def send_own(lo, hi, to_left, to_right):
        for cc in range(lo, hi):
            @pl.when(to_left)
            def _():
                go_left(v, cc, th_at(cc)).start()

            @pl.when(to_right)
            def _():
                go_right(v, cc, th_at(cc)).start()

    send_own(0, M, v > 0, v < V - 1)
    send_own(M, NC, (v > 0) & jnp.logical_not(late_left), (v < V - 1) & jnp.logical_not(late_right))

    def w_at(tt, hh, cw):
        return wbuf.at[pl.ds(pl.multiple_of(tt * F + hh * half + cw * wc, wc), wc)]

    def go_x(k, cw):
        to = lax.rem(t + k, T)
        src = sw.at[pl.ds(pl.multiple_of(g * half + cw * wc, wc), wc)]
        return remote(src, w_at(t, g, cw), x_send.at[to], x_recv.at[k - 1, cw], did(tt=to))

    def go_y(tt, cw):
        return remote(w_at(tt, g, cw), w_at(tt, g, cw), y_send.at[tt], y_recv.at[tt], did(gg=1 - g))

    def x_wait(k, tt, cw):
        remote(w_at(tt, g, cw), w_at(tt, g, cw), x_send.at[tt], x_recv.at[k - 1, cw], did(tt=tt)).wait_recv()

    def w_half(tt, hh):
        return wbuf.at[pl.ds(pl.multiple_of(tt * F + hh * half, half), half)]

    def all_x(k):
        to = lax.rem(t + k, T)
        return remote(w_half(t, g), w_half(t, g), x_send.at[to], x_recv.at[0, 0], did(tt=to))

    def all_y(k, hh):
        tt = lax.rem(t + k, T)
        return remote(w_half(tt, hh), w_half(tt, hh), y_send.at[tt], y_recv.at[tt], did(gg=1 - g))

    nev = (T - 1) * CW
    each(0, nev, lambda j: go_x(j // CW + 1, lax.rem(j, CW)).start())
    for cc in range(NC):
        go_sib(v, cc, th_at(cc)).start()

    def pass_on(j):
        tt = lax.rem(t + T - 1 - j // CW, T)
        cw = lax.rem(j, CW)
        x_wait(j // CW + 1, tt, cw)
        go_y(tt, cw).start()

    for load in loads:
        load.wait()
    hid = sh[...].astype(jnp.float32)
    inverse = lax.rsqrt(jnp.mean(hid * hid, axis=1, keepdims=True) + epsilon)
    normed[...] = (hid * inverse * gain[...]).astype(jnp.bfloat16)

    def multiply(o, cc):
        x = tbuf[cc, pl.ds(o * S, S)].reshape(S * R, fc)
        acc[o, cc // C] += jnp.dot(x, twv[lax.rem(cc, C)], preferred_element_type=jnp.float32)

    def go_acc(o, h):
        p = lax.rem(o, per)
        return remote(acc.at[o, h], tin.at[t, p, h], acc_send, acc_recv.at[t], did(tt=o // per))

    def finished(o, cc):
        @pl.when((lax.rem(cc, C) == C - 1) & (o // per != t))
        def _():
            go_acc(o, cc // C).start()

    acc[...] = jnp.zeros_like(acc)

    pltpu.make_async_copy(tbuf.at[:, me], tbuf.at[:, me], own_sem).wait()
    pltpu.make_async_copy(twv, twv, tw_sem).wait()

    def own_chunk(c):
        other = tbuf.at[c, v * S + 1 - s]
        remote(other, other, sib_send, s_recv.at[v, c], did(ss=1 - s)).wait_recv()
        multiply(v, c)
        finished(v, c)

    spread_own = V > 2
    if not spread_own:
        each(0, NC, own_chunk)

    def take(o, c, slot, onward, has_next):
        here = tbuf.at[c, o * S + s]
        remote(here, here, sib_send, z_recv.at[slot, c], did(ss=1 - s)).wait_recv()

        @pl.when(has_next)
        def _():
            onward(o, c, here).start()

        go_sib(o, c, here).start()

    def use(o, c):
        other = tbuf.at[c, o * S + 1 - s]
        remote(other, other, sib_send, s_recv.at[o, c], did(ss=1 - s)).wait_recv()
        multiply(o, c)
        finished(o, c)

    lane_n = lax.broadcasted_iota(jnp.int32, (frames, N), 1)
    lane = lax.broadcasted_iota(jnp.int32, (frames, frames), 1)
    sub = lax.broadcasted_iota(jnp.int32, (frames, frames), 0)

    def to_columns(row):
        return jnp.transpose(jnp.broadcast_to(row, (frames, frames)))

    def is_label():
        label_col = to_columns(labels[...].astype(jnp.float32)).astype(jnp.int32)[:, 0:1]
        return (label_col - me * N) == lane_n

    steps = (V - 1) * NC
    stride = max(1, min((steps - 2) // nev, 2 * NC // CW))

    passed = (V - 2) * NC
    at_least = lambda i, a: jnp.minimum(jnp.maximum(i - a + 1, 0), 1)
    turn_left = (1 - at_least(v, 1)) * (1 - at_least(t, 1))
    turn_right = at_least(v, V - 1) * at_least(t, T - 1)

    def source(i, turn):
        j = i
        if M < NC:
            j = i + turn * ((NC - M) * at_least(i, M) - (passed + NC - M) * at_least(i, M + passed))
        return j // NC + 1, lax.rem(j, NC)

    def student_head():
        sw_copy.wait()
        each(1, T, lambda k: all_y(k, 1 - g).wait_recv())
        logits = jnp.dot(normed[...], wbuf[...], preferred_element_type=jnp.float32)
        label_logit = jnp.sum(jnp.where(is_label(), logits, 0.0), axis=1, keepdims=True)
        top = jnp.max(logits, axis=1, keepdims=True)
        total = jnp.sum(jnp.exp(logits - top), axis=1, keepdims=True)
        student_ref[...] = logits
        align_cols = to_columns(align[...].astype(jnp.float32)).astype(jnp.int32) - t * frames
        pick_ref[...] = (align_cols == lane).astype(jnp.bfloat16)
        packed[...] = jnp.where(lane == 3, top, jnp.where(lane == 4, total, jnp.where(lane == 5, label_logit, 0.0)))

    student_at = steps - 4 if nev * stride < steps - 4 else None

    def step(i):
        @pl.when(i < steps)
        def _():
            k, c = source(i, turn_left)

            @pl.when(v + k < V)
            def _():
                take(v + k, c, v + k - 1, go_left, v > 0)

            k, c = source(i, turn_right)

            @pl.when(v - k >= 0)
            def _():
                take(v - k, c, v - k, go_right, v < V - 1)

        if M < NC:
            @pl.when(i == passed - 1)
            def _():
                send_own(M, NC, late_left, late_right)

        j = i // stride - 1

        @pl.when((lax.rem(i, stride) == 0) & (j >= 0) & (j < nev))
        def _():
            pass_on(j)

        if spread_own:
            @pl.when((lax.rem(i, OWN) == OWN - 1) & (i // OWN < NC))
            def _():
                own_chunk(i // OWN)

        if student_at is not None:
            @pl.when(i == student_at)
            def _():
                student_head()

        @pl.when(i > 0)
        def _():
            k, c = source(i - 1, turn_left)

            @pl.when(v + k < V)
            def _():
                use(v + k, c)

            k, c = source(i - 1, turn_right)

            @pl.when(v - k >= 0)
            def _():
                use(v - k, c)

    each(0, steps + 1, step)
    each(min(nev, steps // stride), nev, pass_on)

    if student_at is None:
        student_head()
    student = student_ref[...]
    onehot = is_label()
    def tin_wait(k):
        tt = lax.rem(t + k, T)
        remote(tin.at[tt], tin.at[tt], acc_send, acc_recv.at[tt], did(tt=tt)).wait_recv()

    each(1, T, tin_wait)
    for p in range(per):
        for h in range(H):
            total = acc[t * per + p, h]
            for k in range(1, T):
                total = total + tin[lax.rem(t + k, T), p, h]
            for ss in range(S):
                at = (p * S + ss) * rows + h * R
                bl[at:at + R, :] = total[ss * R:(ss + 1) * R]
    whole = bl[...]
    hi = whole.astype(jnp.bfloat16)
    rest = whole - hi.astype(jnp.float32)
    mid = rest.astype(jnp.bfloat16)
    low = (rest - mid.astype(jnp.float32)).astype(jnp.bfloat16)
    rows_of = lambda piece: jnp.dot(pick_ref[...], piece, preferred_element_type=jnp.float32)
    aligned = (rows_of(low) + rows_of(mid)) + rows_of(hi)
    top_t = jnp.max(aligned, axis=1, keepdims=True)
    exp_t = jnp.exp(aligned - top_t)
    sum_t = jnp.sum(exp_t, axis=1, keepdims=True)
    cross_t = jnp.sum(exp_t * (aligned - student), axis=1, keepdims=True)

    pack = packed[...]
    for i, column in enumerate((top_t, sum_t, cross_t)):
        pack = jnp.where(lane == i, column, pack)
    stats[me] = jnp.transpose(pack)[0:8, :]

    def go_stat(k):
        where, other = vs_peer(k)
        return remote(stats.at[me], stats.at[me], stat_send, stat_recv, where)

    def farthest_first(k):
        high = at_least(v, V // 2)
        return high * k + (1 - high) * (VS - k)

    each(1, VS, lambda k: go_stat(farthest_first(k)).start())

    def peers(buf, send, recv):
        return remote(buf.at[0:VS - 1], buf.at[0:VS - 1], send, recv, did(ss=1 - s))

    def turn_block(b):
        turned[b] = jnp.transpose(wbuf[pl.ds(pl.multiple_of(b * w, w), w), :])

    each(0, VS, turn_block)
    peers(stats, stat_send, stat_recv).wait_recv()
    st = stats[...]
    row = lambda i: st[:, i, :]
    all_t = jnp.max(row(0), axis=0, keepdims=True)
    all_s = jnp.max(row(3), axis=0, keepdims=True)
    scale_t = jnp.exp(row(0) - all_t)
    scale_s = jnp.exp(row(3) - all_s)
    add = lambda x: jnp.sum(x, axis=0, keepdims=True)
    total_t = add(row(1) * scale_t)
    lse_t = all_t + jnp.log(total_t)
    lse_s = all_s + jnp.log(add(row(4) * scale_s))
    mask_float = mask[...].astype(jnp.float32)
    mask_count = jnp.sum(jnp.sum(mask_float, axis=1, keepdims=True), axis=0, keepdims=True)
    own_mask = mask[pl.ds(t, 1), :].astype(jnp.float32)
    row_weight = own_mask * (T * frames) / mask_count
    unpacked = jnp.where(sub == 0, lse_t, jnp.where(sub == 1, lse_s, row_weight))
    columns = jnp.transpose(unpacked)
    teacher_prob = jnp.exp(aligned - columns[:, 0:1])
    student_prob = jnp.exp(student - columns[:, 1:2])
    grad = (
        loss_scale * columns[:, 2:3]
        * ((1.0 + label_weight) * student_prob - teacher_prob - label_weight * onehot.astype(jnp.float32))
    ).astype(jnp.bfloat16)
    lg_out[...] = grad
    stores = [
        pltpu.make_async_copy(source, target, out_sem.at[i])
        for i, (source, target) in enumerate((
            (rl_out, rl_hbm),
            (lg_out, out_hbm.at[:, 0:N]),
            (hg_out, out_hbm.at[:, N:]),
        ))
    ]

    def go_inner(k):
        where, other = vs_peer(k)
        return remote(inner_in.at[me], inner_in.at[me], inner_send, inner_recv, where)

    def term(block):
        return jnp.dot(lg_out[...], turned[block], preferred_element_type=jnp.float32)

    def piece(buf, b, p):
        return buf.at[b, pl.ds(pl.multiple_of(p * rp, rp), rp)]

    def go_gs(b, p):
        return remote(piece(sibout, b, p), piece(sibin, b, p), gs_send, gs_recv.at[b, p], did(ss=1 - s))

    def order(q):
        b = lax.rem(q, 2) * (q // 2) + (1 - lax.rem(q, 2)) * (V - 1 - q // 2)
        high = at_least(v, V // 2)
        return high * (V - 1 - b) + (1 - high) * b

    def first_sib(p):
        b = order(0)
        at = pl.ds(pl.multiple_of(p * rp, rp), rp)
        sibout[b, at] = jnp.dot(lg_out[at, :], turned[b * S + 1 - s], preferred_element_type=jnp.float32)
        go_gs(b, p).start()

    def for_sib(q):
        b = order(q)
        sibout[b] = term(b * S + 1 - s)
        each(0, RP, lambda p: go_gs(b, p).start())

    def for_own(q):
        b = order(q)
        part[b] = term(b * S + s)

    def go_line(buf, turn, b, p, onward):
        return remote(piece(part, b, p), piece(buf, b, p), ln_send, ln_recv.at[b + turn, p], did(vv=onward))

    def line(n, buf, turn, b_of, comes, onward):
        q, p = n // RP, lax.rem(n, RP)
        b = b_of(q)

        at = pl.ds(pl.multiple_of(p * rp, rp), rp)
        go_gs(b, p).wait_recv()
        part[b, at] += sibin[b, at]

        @pl.when(comes)
        def _():
            go_line(buf, turn, b, p, onward).wait_recv()
            part[b, at] += buf[b, at]

        go_line(buf, turn, b, p, onward).start()

    from_top, from_zero = (lambda q: V - 1 - q), (lambda q: q)

    def line_step(i):
        n = i - v * LAG

        @pl.when((n >= 0) & (n < (V - 1 - v) * RP))
        def _():
            line(n, rin, 1, from_top, v > 0, v + 1)

        m = i - (V - 1 - v) * LAG

        @pl.when((m >= 0) & (m < v * RP))
        def _():
            line(m, lin, 0, from_zero, v < V - 1, v - 1)

    each(0, RP, first_sib)
    stores[1].start()
    for_own(0)
    for_sib(1)
    diverge = add(row(2) * scale_t) / total_t - lse_t + lse_s
    cross_term = lse_s - add(row(5))
    rl_out[...] = row_weight * (diverge + label_weight * cross_term)
    stores[0].start()
    inner = jnp.sum(lg_out[...].astype(jnp.float32) * student_ref[...], axis=1, keepdims=True)
    inner_in[me] = jnp.transpose(jnp.broadcast_to(inner, (frames, frames)))[0:8, :]
    each(0, LAG, line_step)
    for_own(1)
    each(2, V, for_sib)
    each(2, V, for_own)
    each(1, VS, lambda k: go_inner(k).start())
    each(LAG, (V - 1) * max(RP, LAG), line_step)

    inside = (v > 0) & (v < V - 1)

    def z_sent(planes):
        some = tbuf.at[:, 0:planes]
        remote(some, some, z_send, z_recv.at[0, 0], did(ss=1 - s)).wait_send()

    @pl.when(inside)
    def _():
        z_sent(V + 1)

    @pl.when(jnp.logical_not(inside))
    def _():
        z_sent(1)

    section = tbuf.at[:, 0:V]
    remote(section, section, sib_send, s_recv.at[0, 0], did(ss=1 - s)).wait_send()
    others = acc.at[0:V - per]
    remote(others, others, acc_send, acc_recv.at[t], did(ss=1 - s)).wait_send()

    def w_sent(k):
        all_x(k).wait_send()
        all_y(k, g).wait_send()

    each(1, T, w_sent)
    remote(sibout, sibout, gs_send, gs_recv.at[0, 0], did(ss=1 - s)).wait_send()
    peers(stats, stat_send, stat_recv).wait_send()
    peers(inner_in, inner_send, inner_recv).wait_send()
    peers(inner_in, inner_send, inner_recv).wait_recv()
    inner_total = jnp.sum(inner_in[...], axis=0)[0:1, :]
    inner_rows = to_columns(inner_total)[:, 0:1]

    each(0, RP, lambda p: go_gs(v, p).wait_recv())
    part[v] += sibin[v]

    def last(buf, turn, onward):
        each(0, RP, lambda p: go_line(buf, turn, v, p, onward).wait_recv())
        part[v] += buf[v]

    @pl.when(v > 0)
    def _():
        last(rin, 1, v - 1)

    @pl.when(v < V - 1)
    def _():
        last(lin, 0, v + 1)

    mine = pl.multiple_of(me * w, w)
    scaled = part[v] * gain[:, pl.ds(mine, w)]
    own_hidden = sh[:, pl.ds(mine, w)].astype(jnp.float32)
    hg_out[...] = (inverse * scaled - own_hidden * (inverse**2 * inner_rows / DS)).astype(jnp.bfloat16)

    stores[2].start()

    some = part.at[0:V - 1]
    remote(some, some, ln_send, ln_recv.at[0, 0], did(ss=1 - s)).wait_send()
    for store in stores:
        store.wait()


def spread(loss_in, both_in, loss_hbm, grad_hbm, hidden_hbm, loss, grad, hidden, sem):
    N = grad.shape[1]
    loads = [
        pltpu.make_async_copy(source, target, sem.at[i])
        for i, (source, target) in enumerate(
            ((both_in.at[:, 0:N], grad), (both_in.at[:, N:], hidden), (loss_in, loss))
        )
    ]
    stores = [
        pltpu.make_async_copy(source, target, sem.at[i])
        for i, (source, target) in enumerate(((grad, grad_hbm), (hidden, hidden_hbm), (loss, loss_hbm)))
    ]
    for load in loads:
        load.start()
    for load, store in zip(loads, stores):
        load.wait()
        store.start()
    for store in stores:
        store.wait()


def local(sizes, teacher_hidden, teacher_weight, student_hidden, student_gain, student_weight, labels, alignment, loss_mask):
    G, V, T, S, H, C, CW, RP, LAG, M, OWN = sizes
    VS = V * S
    NC = H * C
    rows, width = teacher_hidden.shape
    R = rows // H
    fc = width // C
    N = teacher_weight.shape[1]
    frames, DS = student_hidden.shape
    w = DS // VS
    per = V // T
    f32, bf16 = jnp.float32, jnp.bfloat16
    dma = pltpu.SemaphoreType.DMA
    hbm = pl.BlockSpec(memory_space=pl.ANY)
    row_loss, both = pl.pallas_call(
        functools.partial(kernel, sizes),
        out_shape=(jax.ShapeDtypeStruct((1, frames), f32), jax.ShapeDtypeStruct((frames, N + w), bf16)),
        in_specs=[hbm] * 8,
        out_specs=(hbm, hbm),
        scratch_shapes=[
            pltpu.VMEM((frames, DS), bf16),
            pltpu.VMEM((1, DS), f32),
            pltpu.VMEM((1, frames), jnp.int32),
            pltpu.VMEM((1, frames), jnp.int32),
            pltpu.VMEM((T, frames), jnp.int32),
            pltpu.VMEM((1, frames), f32),
            pltpu.VMEM((frames, N), bf16),
            pltpu.VMEM((frames, w), bf16),
            pltpu.VMEM((NC, VS, R, fc), bf16),
            pltpu.VMEM((C, fc, N), bf16),
            pltpu.VMEM((DS, N), bf16),
            pltpu.VMEM((frames, DS), bf16),
            pltpu.VMEM((V, H, S * R, N), f32),
            pltpu.VMEM((T, per, H, S * R, N), f32),
            pltpu.VMEM((frames, N), f32),
            pltpu.VMEM((VS, 8, frames), f32),
            pltpu.VMEM((VS, 8, frames), f32),
            pltpu.VMEM((V, frames, w), f32),
            pltpu.VMEM((V, frames, w), f32),
            pltpu.VMEM((V, frames, w), f32),
            pltpu.VMEM((V, frames, w), f32),
            pltpu.VMEM((V, frames, w), f32),
            pltpu.VMEM((frames, N), f32),
            pltpu.VMEM((frames, frames), f32),
            pltpu.VMEM((VS, N, w), bf16),
            pltpu.VMEM((frames, frames), bf16),
            dma, dma, dma, dma((5,)), dma((3,)),
            dma, dma, dma((V - 1, NC)), dma((V, NC)),
            dma((T,)), dma((T - 1, CW)), dma((T,)), dma((T,)),
            dma, dma((T,)),
            dma, dma, dma, dma,
            dma, dma((V, RP)), dma, dma((V + 1, RP)),
        ],
        compiler_params=pltpu.CompilerParams(
            collective_id=0, has_side_effects=True, vmem_limit_bytes=63 * 2**20
        ),
    )(
        teacher_hidden, teacher_weight, student_hidden, student_gain.reshape(1, DS), student_weight,
        labels.reshape(1, frames), alignment.reshape(1, frames), loss_mask.reshape(T, frames),
    )
    row_loss, logit_grad, hidden_grad = pl.pallas_call(
        spread,
        out_shape=(
            jax.ShapeDtypeStruct((1, frames), f32),
            jax.ShapeDtypeStruct((frames, N), bf16),
            jax.ShapeDtypeStruct((frames, w), bf16),
        ),
        in_specs=[hbm] * 2,
        out_specs=(hbm,) * 3,
        scratch_shapes=[pltpu.VMEM((1, frames), f32), pltpu.VMEM((frames, N), bf16), pltpu.VMEM((frames, w), bf16), dma((3,))],
    )(row_loss, both)
    return row_loss.reshape(frames), logit_grad, hidden_grad


def solution(mesh):
    sizes = tuple(mesh.shape[a] for a in ("groups", "vocab", "tokens", "section")) + (2, 4, 8, 2, 1, 4, 2)
    in_specs = (
        P(("groups", "vocab", "section"), "tokens"),
        P("tokens", ("vocab", "section")),
        P(("groups", "tokens"), None),
        P(),
        P("tokens", ("vocab", "section")),
        P(("groups", "tokens")),
        P(("groups", "tokens")),
        P("groups"),
    )
    out_specs = (
        P(("groups", "tokens")),
        P(("groups", "tokens"), ("vocab", "section")),
        P(("groups", "tokens"), ("vocab", "section")),
    )
    return jax.shard_map(
        functools.partial(local, sizes), mesh=mesh, in_specs=in_specs, out_specs=out_specs, check_vma=False
    )
```

```python
import functools

import jax
import jax.numpy as jnp
from jax import lax
from jax.experimental import pallas as pl
from jax.experimental.pallas import tpu as pltpu
from jax.sharding import PartitionSpec as P

label_weight = 0.2
loss_scale = 16.0
epsilon = 1e-05
MESH = pl.DeviceIdType.MESH


def kernel(
    sizes, th, tw, sh_in, gain_in, sw, labels_in, align_in, mask_in,
    rl_hbm, out_hbm,
    sh, gain, labels, align, mask, rl_out, lg_out, hg_out,
    tbuf, twv, wbuf, normed, acc, tin, bl, stats, inner_in, sibout, sibin, part, rin, lin, student_ref, packed, turned, pick_ref,
    tw_sem, own_sem, sw_sem, in_sem, out_sem,
    z_send, sib_send, z_recv, s_recv,
    x_send, x_recv, y_send, y_recv,
    acc_send, acc_recv,
    stat_send, stat_recv, inner_send, inner_recv,
    gs_send, gs_recv, ln_send, ln_recv,
):
    G, V, T, S, H, C, CW, RP, LAG, M, OWN = sizes
    NC = H * C
    VS = V * S
    M = M if T == 2 and V > 2 else NC
    g, v, t, s = (lax.axis_index(a) for a in ("groups", "vocab", "tokens", "section"))
    me = v * S + s
    rows = th.shape[0]
    R = rows // H
    fc = th.shape[1] // C
    F = sw.shape[0]
    half = F // 2
    wc = half // CW
    frames, DS = sh.shape
    N = tw.shape[1]
    w = DS // VS
    per = V // T
    rp = frames // RP

    def did(gg=None, vv=None, tt=None, ss=None):
        pick = lambda a, b: b if a is None else a
        return (pick(gg, g), pick(vv, v), pick(tt, t), pick(ss, s))

    def remote(src, dst, send, recv, where):
        return pltpu.make_async_remote_copy(
            src_ref=src, dst_ref=dst, send_sem=send, recv_sem=recv,
            device_id=where, device_id_type=MESH,
        )

    def vs_peer(k):
        other = lax.rem(me + k, VS)
        return did(vv=other // S, ss=lax.rem(other, S)), other

    def each(lo, hi, body):
        def run(i, carry):
            body(i)
            return carry
        lax.fori_loop(lo, hi, run, 0)

    barrier = pltpu.get_barrier_semaphore()

    def greet(where):
        pl.semaphore_signal(barrier, inc=1, device_id=where, device_id_type=MESH)

    loads = [
        pltpu.make_async_copy(source, target, in_sem.at[i])
        for i, (source, target) in enumerate(
            ((sh_in, sh), (gain_in, gain), (labels_in, labels), (align_in, align), (mask_in, mask))
        )
    ]
    for load in loads:
        load.start()
    def th_at(cc):
        h, c = cc // C, cc % C
        return th.at[h * R:(h + 1) * R, c * fc:(c + 1) * fc]

    for c in range(C):
        pltpu.make_async_copy(tw.at[c * fc:(c + 1) * fc], twv.at[c], tw_sem).start()
    for cc in range(NC):
        pltpu.make_async_copy(th_at(cc), tbuf.at[cc, me], own_sem).start()
    sw_copy = pltpu.make_async_copy(sw, wbuf.at[pl.ds(pl.multiple_of(t * F, F), F)], sw_sem)
    sw_copy.start()

    each(1, VS, lambda k: greet(vs_peer(k)[0]))
    each(1, T, lambda k: greet(did(tt=lax.rem(t + k, T))))
    greet(did(gg=1 - g))
    pl.semaphore_wait(barrier, VS - 1 + T - 1 + 1)

    def go_left(o, c, src):
        return remote(src, tbuf.at[c, o * S + s], z_send, z_recv.at[o - 1, c], did(vv=v - 1))

    def go_right(o, c, src):
        return remote(src, tbuf.at[c, o * S + s], z_send, z_recv.at[o, c], did(vv=v + 1))

    def go_sib(o, c, src):
        return remote(src, tbuf.at[c, o * S + s], sib_send, s_recv.at[o, c], did(ss=1 - s))

    late_left = (v == 1) & (t == 0)
    late_right = (v == V - 2) & (t == T - 1)

    def send_own(lo, hi, to_left, to_right):
        for cc in range(lo, hi):
            @pl.when(to_left)
            def _():
                go_left(v, cc, th_at(cc)).start()

            @pl.when(to_right)
            def _():
                go_right(v, cc, th_at(cc)).start()

    send_own(0, M, v > 0, v < V - 1)
    send_own(M, NC, (v > 0) & jnp.logical_not(late_left), (v < V - 1) & jnp.logical_not(late_right))

    def w_at(tt, hh, cw):
        return wbuf.at[pl.ds(pl.multiple_of(tt * F + hh * half + cw * wc, wc), wc)]

    def go_x(k, cw):
        to = lax.rem(t + k, T)
        src = sw.at[pl.ds(pl.multiple_of(g * half + cw * wc, wc), wc)]
        return remote(src, w_at(t, g, cw), x_send.at[to], x_recv.at[k - 1, cw], did(tt=to))

    def go_y(tt, cw):
        return remote(w_at(tt, g, cw), w_at(tt, g, cw), y_send.at[tt], y_recv.at[tt], did(gg=1 - g))

    def x_wait(k, tt, cw):
        remote(w_at(tt, g, cw), w_at(tt, g, cw), x_send.at[tt], x_recv.at[k - 1, cw], did(tt=tt)).wait_recv()

    def w_half(tt, hh):
        return wbuf.at[pl.ds(pl.multiple_of(tt * F + hh * half, half), half)]

    def all_x(k):
        to = lax.rem(t + k, T)
        return remote(w_half(t, g), w_half(t, g), x_send.at[to], x_recv.at[0, 0], did(tt=to))

    def all_y(k, hh):
        tt = lax.rem(t + k, T)
        return remote(w_half(tt, hh), w_half(tt, hh), y_send.at[tt], y_recv.at[tt], did(gg=1 - g))

    nev = (T - 1) * CW
    each(0, nev, lambda j: go_x(j // CW + 1, lax.rem(j, CW)).start())
    for cc in range(NC):
        go_sib(v, cc, th_at(cc)).start()

    def pass_on(j):
        tt = lax.rem(t + T - 1 - j // CW, T)
        cw = lax.rem(j, CW)
        x_wait(j // CW + 1, tt, cw)
        go_y(tt, cw).start()

    for load in loads:
        load.wait()
    hid = sh[...].astype(jnp.float32)
    inverse = lax.rsqrt(jnp.mean(hid * hid, axis=1, keepdims=True) + epsilon)
    normed[...] = (hid * inverse * gain[...]).astype(jnp.bfloat16)

    def multiply(o, cc):
        x = tbuf[cc, pl.ds(o * S, S)].reshape(S * R, fc)
        acc[o, cc // C] += jnp.dot(x, twv[lax.rem(cc, C)], preferred_element_type=jnp.float32)

    def go_acc(o, h):
        p = lax.rem(o, per)
        return remote(acc.at[o, h], tin.at[t, p, h], acc_send, acc_recv.at[t], did(tt=o // per))

    def finished(o, cc):
        @pl.when((lax.rem(cc, C) == C - 1) & (o // per != t))
        def _():
            go_acc(o, cc // C).start()

    acc[...] = jnp.zeros_like(acc)

    pltpu.make_async_copy(tbuf.at[:, me], tbuf.at[:, me], own_sem).wait()
    pltpu.make_async_copy(twv, twv, tw_sem).wait()

    def own_chunk(c):
        other = tbuf.at[c, v * S + 1 - s]
        remote(other, other, sib_send, s_recv.at[v, c], did(ss=1 - s)).wait_recv()
        multiply(v, c)
        finished(v, c)

    spread_own = V > 2
    if not spread_own:
        each(0, NC, own_chunk)

    def take(o, c, slot, onward, has_next):
        here = tbuf.at[c, o * S + s]
        remote(here, here, sib_send, z_recv.at[slot, c], did(ss=1 - s)).wait_recv()

        @pl.when(has_next)
        def _():
            onward(o, c, here).start()

        go_sib(o, c, here).start()

    def use(o, c):
        other = tbuf.at[c, o * S + 1 - s]
        remote(other, other, sib_send, s_recv.at[o, c], did(ss=1 - s)).wait_recv()
        multiply(o, c)
        finished(o, c)

    lane_n = lax.broadcasted_iota(jnp.int32, (frames, N), 1)
    lane = lax.broadcasted_iota(jnp.int32, (frames, frames), 1)
    sub = lax.broadcasted_iota(jnp.int32, (frames, frames), 0)

    def to_columns(row):
        return jnp.transpose(jnp.broadcast_to(row, (frames, frames)))

    def is_label():
        label_col = to_columns(labels[...].astype(jnp.float32)).astype(jnp.int32)[:, 0:1]
        return (label_col - me * N) == lane_n

    steps = (V - 1) * NC
    stride = max(1, min((steps - 2) // nev, 2 * NC // CW))

    passed = (V - 2) * NC
    at_least = lambda i, a: jnp.minimum(jnp.maximum(i - a + 1, 0), 1)
    turn_left = (1 - at_least(v, 1)) * (1 - at_least(t, 1))
    turn_right = at_least(v, V - 1) * at_least(t, T - 1)

    def source(i, turn):
        j = i
        if M < NC:
            j = i + turn * ((NC - M) * at_least(i, M) - (passed + NC - M) * at_least(i, M + passed))
        return j // NC + 1, lax.rem(j, NC)

    def student_head():
        sw_copy.wait()
        each(1, T, lambda k: all_y(k, 1 - g).wait_recv())
        logits = jnp.dot(normed[...], wbuf[...], preferred_element_type=jnp.float32)
        label_logit = jnp.sum(jnp.where(is_label(), logits, 0.0), axis=1, keepdims=True)
        top = jnp.max(logits, axis=1, keepdims=True)
        total = jnp.sum(jnp.exp(logits - top), axis=1, keepdims=True)
        student_ref[...] = logits
        align_cols = to_columns(align[...].astype(jnp.float32)).astype(jnp.int32) - t * frames
        pick_ref[...] = (align_cols == lane).astype(jnp.bfloat16)
        packed[...] = jnp.where(lane == 3, top, jnp.where(lane == 4, total, jnp.where(lane == 5, label_logit, 0.0)))

    student_at = steps - 4 if nev * stride < steps - 4 else None

    def step(i):
        @pl.when(i < steps)
        def _():
            k, c = source(i, turn_left)

            @pl.when(v + k < V)
            def _():
                take(v + k, c, v + k - 1, go_left, v > 0)

            k, c = source(i, turn_right)

            @pl.when(v - k >= 0)
            def _():
                take(v - k, c, v - k, go_right, v < V - 1)

        if M < NC:
            @pl.when(i == passed - 1)
            def _():
                send_own(M, NC, late_left, late_right)

        j = i // stride - 1

        @pl.when((lax.rem(i, stride) == 0) & (j >= 0) & (j < nev))
        def _():
            pass_on(j)

        if spread_own:
            @pl.when((lax.rem(i, OWN) == OWN - 1) & (i // OWN < NC))
            def _():
                own_chunk(i // OWN)

        if student_at is not None:
            @pl.when(i == student_at)
            def _():
                student_head()

        @pl.when(i > 0)
        def _():
            k, c = source(i - 1, turn_left)

            @pl.when(v + k < V)
            def _():
                use(v + k, c)

            k, c = source(i - 1, turn_right)

            @pl.when(v - k >= 0)
            def _():
                use(v - k, c)

    each(0, steps + 1, step)
    each(min(nev, steps // stride), nev, pass_on)

    if student_at is None:
        student_head()
    student = student_ref[...]
    onehot = is_label()
    def tin_wait(k):
        tt = lax.rem(t + k, T)
        remote(tin.at[tt], tin.at[tt], acc_send, acc_recv.at[tt], did(tt=tt)).wait_recv()

    each(1, T, tin_wait)
    for p in range(per):
        for h in range(H):
            total = acc[t * per + p, h]
            for k in range(1, T):
                total = total + tin[lax.rem(t + k, T), p, h]
            for ss in range(S):
                at = (p * S + ss) * rows + h * R
                bl[at:at + R, :] = total[ss * R:(ss + 1) * R]
    whole = bl[...]
    hi = whole.astype(jnp.bfloat16)
    rest = whole - hi.astype(jnp.float32)
    mid = rest.astype(jnp.bfloat16)
    low = (rest - mid.astype(jnp.float32)).astype(jnp.bfloat16)
    rows_of = lambda piece: jnp.dot(pick_ref[...], piece, preferred_element_type=jnp.float32)
    aligned = (rows_of(low) + rows_of(mid)) + rows_of(hi)
    top_t = jnp.max(aligned, axis=1, keepdims=True)
    exp_t = jnp.exp(aligned - top_t)
    sum_t = jnp.sum(exp_t, axis=1, keepdims=True)
    cross_t = jnp.sum(exp_t * (aligned - student), axis=1, keepdims=True)

    pack = packed[...]
    for i, column in enumerate((top_t, sum_t, cross_t)):
        pack = jnp.where(lane == i, column, pack)
    stats[me] = jnp.transpose(pack)[0:8, :]

    def go_stat(k):
        where, other = vs_peer(k)
        return remote(stats.at[me], stats.at[me], stat_send, stat_recv, where)

    def farthest_first(k):
        high = at_least(v, V // 2)
        return high * k + (1 - high) * (VS - k)

    each(1, VS, lambda k: go_stat(farthest_first(k)).start())

    def peers(buf, send, recv):
        return remote(buf.at[0:VS - 1], buf.at[0:VS - 1], send, recv, did(ss=1 - s))

    def turn_block(b):
        turned[b] = jnp.transpose(wbuf[pl.ds(pl.multiple_of(b * w, w), w), :])

    each(0, VS, turn_block)
    peers(stats, stat_send, stat_recv).wait_recv()
    st = stats[...]
    row = lambda i: st[:, i, :]
    all_t = jnp.max(row(0), axis=0, keepdims=True)
    all_s = jnp.max(row(3), axis=0, keepdims=True)
    scale_t = jnp.exp(row(0) - all_t)
    scale_s = jnp.exp(row(3) - all_s)
    add = lambda x: jnp.sum(x, axis=0, keepdims=True)
    total_t = add(row(1) * scale_t)
    lse_t = all_t + jnp.log(total_t)
    lse_s = all_s + jnp.log(add(row(4) * scale_s))
    mask_float = mask[...].astype(jnp.float32)
    mask_count = jnp.sum(jnp.sum(mask_float, axis=1, keepdims=True), axis=0, keepdims=True)
    own_mask = mask[pl.ds(t, 1), :].astype(jnp.float32)
    row_weight = own_mask * (T * frames) / mask_count
    unpacked = jnp.where(sub == 0, lse_t, jnp.where(sub == 1, lse_s, row_weight))
    columns = jnp.transpose(unpacked)
    teacher_prob = jnp.exp(aligned - columns[:, 0:1])
    student_prob = jnp.exp(student - columns[:, 1:2])
    grad = (
        loss_scale * columns[:, 2:3]
        * ((1.0 + label_weight) * student_prob - teacher_prob - label_weight * onehot.astype(jnp.float32))
    ).astype(jnp.bfloat16)
    lg_out[...] = grad
    stores = [
        pltpu.make_async_copy(source, target, out_sem.at[i])
        for i, (source, target) in enumerate((
            (rl_out, rl_hbm),
            (lg_out, out_hbm.at[:, 0:N]),
            (hg_out, out_hbm.at[:, N:]),
        ))
    ]

    def go_inner(k):
        where, other = vs_peer(k)
        return remote(inner_in.at[me], inner_in.at[me], inner_send, inner_recv, where)

    def term(block):
        return jnp.dot(lg_out[...], turned[block], preferred_element_type=jnp.float32)

    def piece(buf, b, p):
        return buf.at[b, pl.ds(pl.multiple_of(p * rp, rp), rp)]

    def go_gs(b, p):
        return remote(piece(sibout, b, p), piece(sibin, b, p), gs_send, gs_recv.at[b, p], did(ss=1 - s))

    def order(q):
        b = lax.rem(q, 2) * (q // 2) + (1 - lax.rem(q, 2)) * (V - 1 - q // 2)
        high = at_least(v, V // 2)
        return high * (V - 1 - b) + (1 - high) * b

    def first_sib(p):
        b = order(0)
        at = pl.ds(pl.multiple_of(p * rp, rp), rp)
        sibout[b, at] = jnp.dot(lg_out[at, :], turned[b * S + 1 - s], preferred_element_type=jnp.float32)
        go_gs(b, p).start()

    def for_sib(q):
        b = order(q)
        sibout[b] = term(b * S + 1 - s)
        each(0, RP, lambda p: go_gs(b, p).start())

    def for_own(q):
        b = order(q)
        part[b] = term(b * S + s)

    def go_line(buf, turn, b, p, onward):
        return remote(piece(part, b, p), piece(buf, b, p), ln_send, ln_recv.at[b + turn, p], did(vv=onward))

    def line(n, buf, turn, b_of, comes, onward):
        q, p = n // RP, lax.rem(n, RP)
        b = b_of(q)

        at = pl.ds(pl.multiple_of(p * rp, rp), rp)
        go_gs(b, p).wait_recv()
        part[b, at] += sibin[b, at]

        @pl.when(comes)
        def _():
            go_line(buf, turn, b, p, onward).wait_recv()
            part[b, at] += buf[b, at]

        go_line(buf, turn, b, p, onward).start()

    from_top, from_zero = (lambda q: V - 1 - q), (lambda q: q)

    def line_step(i):
        n = i - v * LAG

        @pl.when((n >= 0) & (n < (V - 1 - v) * RP))
        def _():
            line(n, rin, 1, from_top, v > 0, v + 1)

        m = i - (V - 1 - v) * LAG

        @pl.when((m >= 0) & (m < v * RP))
        def _():
            line(m, lin, 0, from_zero, v < V - 1, v - 1)

    each(0, RP, first_sib)
    stores[1].start()
    for_own(0)
    for_sib(1)
    diverge = add(row(2) * scale_t) / total_t - lse_t + lse_s
    cross_term = lse_s - add(row(5))
    rl_out[...] = row_weight * (diverge + label_weight * cross_term)
    stores[0].start()
    inner = jnp.sum(lg_out[...].astype(jnp.float32) * student_ref[...], axis=1, keepdims=True)
    inner_in[me] = jnp.transpose(jnp.broadcast_to(inner, (frames, frames)))[0:8, :]
    each(0, LAG, line_step)
    for_own(1)
    each(2, V, for_sib)
    each(2, V, for_own)
    each(1, VS, lambda k: go_inner(k).start())
    each(LAG, (V - 1) * max(RP, LAG), line_step)

    inside = (v > 0) & (v < V - 1)

    def z_sent(planes):
        some = tbuf.at[:, 0:planes]
        remote(some, some, z_send, z_recv.at[0, 0], did(ss=1 - s)).wait_send()

    @pl.when(inside)
    def _():
        z_sent(V + 1)

    @pl.when(jnp.logical_not(inside))
    def _():
        z_sent(1)

    section = tbuf.at[:, 0:V]
    remote(section, section, sib_send, s_recv.at[0, 0], did(ss=1 - s)).wait_send()
    others = acc.at[0:V - per]
    remote(others, others, acc_send, acc_recv.at[t], did(ss=1 - s)).wait_send()

    def w_sent(k):
        all_x(k).wait_send()
        all_y(k, g).wait_send()

    each(1, T, w_sent)
    remote(sibout, sibout, gs_send, gs_recv.at[0, 0], did(ss=1 - s)).wait_send()
    peers(stats, stat_send, stat_recv).wait_send()
    peers(inner_in, inner_send, inner_recv).wait_send()
    peers(inner_in, inner_send, inner_recv).wait_recv()
    inner_total = jnp.sum(inner_in[...], axis=0)[0:1, :]
    inner_rows = to_columns(inner_total)[:, 0:1]

    each(0, RP, lambda p: go_gs(v, p).wait_recv())
    part[v] += sibin[v]

    def last(buf, turn, onward):
        each(0, RP, lambda p: go_line(buf, turn, v, p, onward).wait_recv())
        part[v] += buf[v]

    @pl.when(v > 0)
    def _():
        last(rin, 1, v - 1)

    @pl.when(v < V - 1)
    def _():
        last(lin, 0, v + 1)

    mine = pl.multiple_of(me * w, w)
    scaled = part[v] * gain[:, pl.ds(mine, w)]
    own_hidden = sh[:, pl.ds(mine, w)].astype(jnp.float32)
    hg_out[...] = (inverse * scaled - own_hidden * (inverse**2 * inner_rows / DS)).astype(jnp.bfloat16)

    stores[2].start()

    some = part.at[0:V - 1]
    remote(some, some, ln_send, ln_recv.at[0, 0], did(ss=1 - s)).wait_send()
    for store in stores:
        store.wait()


def spread(loss_in, both_in, loss_hbm, grad_hbm, hidden_hbm, loss, grad, hidden, sem):
    N = grad.shape[1]
    loads = [
        pltpu.make_async_copy(source, target, sem.at[i])
        for i, (source, target) in enumerate(
            ((both_in.at[:, 0:N], grad), (both_in.at[:, N:], hidden), (loss_in, loss))
        )
    ]
    stores = [
        pltpu.make_async_copy(source, target, sem.at[i])
        for i, (source, target) in enumerate(((grad, grad_hbm), (hidden, hidden_hbm), (loss, loss_hbm)))
    ]
    for load in loads:
        load.start()
    for load, store in zip(loads, stores):
        load.wait()
        store.start()
    for store in stores:
        store.wait()


def local(sizes, teacher_hidden, teacher_weight, student_hidden, student_gain, student_weight, labels, alignment, loss_mask):
    G, V, T, S, H, C, CW, RP, LAG, M, OWN = sizes
    VS = V * S
    NC = H * C
    rows, width = teacher_hidden.shape
    R = rows // H
    fc = width // C
    N = teacher_weight.shape[1]
    frames, DS = student_hidden.shape
    w = DS // VS
    per = V // T
    f32, bf16 = jnp.float32, jnp.bfloat16
    dma = pltpu.SemaphoreType.DMA
    hbm = pl.BlockSpec(memory_space=pl.ANY)
    row_loss, both = pl.pallas_call(
        functools.partial(kernel, sizes),
        out_shape=(jax.ShapeDtypeStruct((1, frames), f32), jax.ShapeDtypeStruct((frames, N + w), bf16)),
        in_specs=[hbm] * 8,
        out_specs=(hbm, hbm),
        scratch_shapes=[
            pltpu.VMEM((frames, DS), bf16),
            pltpu.VMEM((1, DS), f32),
            pltpu.VMEM((1, frames), jnp.int32),
            pltpu.VMEM((1, frames), jnp.int32),
            pltpu.VMEM((T, frames), jnp.int32),
            pltpu.VMEM((1, frames), f32),
            pltpu.VMEM((frames, N), bf16),
            pltpu.VMEM((frames, w), bf16),
            pltpu.VMEM((NC, VS, R, fc), bf16),
            pltpu.VMEM((C, fc, N), bf16),
            pltpu.VMEM((DS, N), bf16),
            pltpu.VMEM((frames, DS), bf16),
            pltpu.VMEM((V, H, S * R, N), f32),
            pltpu.VMEM((T, per, H, S * R, N), f32),
            pltpu.VMEM((frames, N), f32),
            pltpu.VMEM((VS, 8, frames), f32),
            pltpu.VMEM((VS, 8, frames), f32),
            pltpu.VMEM((V, frames, w), f32),
            pltpu.VMEM((V, frames, w), f32),
            pltpu.VMEM((V, frames, w), f32),
            pltpu.VMEM((V, frames, w), f32),
            pltpu.VMEM((V, frames, w), f32),
            pltpu.VMEM((frames, N), f32),
            pltpu.VMEM((frames, frames), f32),
            pltpu.VMEM((VS, N, w), bf16),
            pltpu.VMEM((frames, frames), bf16),
            dma, dma, dma, dma((5,)), dma((3,)),
            dma, dma, dma((V - 1, NC)), dma((V, NC)),
            dma((T,)), dma((T - 1, CW)), dma((T,)), dma((T,)),
            dma, dma((T,)),
            dma, dma, dma, dma,
            dma, dma((V, RP)), dma, dma((V + 1, RP)),
        ],
        compiler_params=pltpu.CompilerParams(
            collective_id=0, has_side_effects=True, vmem_limit_bytes=63 * 2**20
        ),
    )(
        teacher_hidden, teacher_weight, student_hidden, student_gain.reshape(1, DS), student_weight,
        labels.reshape(1, frames), alignment.reshape(1, frames), loss_mask.reshape(T, frames),
    )
    row_loss, logit_grad, hidden_grad = pl.pallas_call(
        spread,
        out_shape=(
            jax.ShapeDtypeStruct((1, frames), f32),
            jax.ShapeDtypeStruct((frames, N), bf16),
            jax.ShapeDtypeStruct((frames, w), bf16),
        ),
        in_specs=[hbm] * 2,
        out_specs=(hbm,) * 3,
        scratch_shapes=[pltpu.VMEM((1, frames), f32), pltpu.VMEM((frames, N), bf16), pltpu.VMEM((frames, w), bf16), dma((3,))],
    )(row_loss, both)
    return row_loss.reshape(frames), logit_grad, hidden_grad


def solution(mesh):
    sizes = tuple(mesh.shape[a] for a in ("groups", "vocab", "tokens", "section")) + (2, 4, 8, 4, 2, 4, 2)
    in_specs = (
        P(("groups", "vocab", "section"), "tokens"),
        P("tokens", ("vocab", "section")),
        P(("groups", "tokens"), None),
        P(),
        P("tokens", ("vocab", "section")),
        P(("groups", "tokens")),
        P(("groups", "tokens")),
        P("groups"),
    )
    out_specs = (
        P(("groups", "tokens")),
        P(("groups", "tokens"), ("vocab", "section")),
        P(("groups", "tokens"), ("vocab", "section")),
    )
    return jax.shard_map(
        functools.partial(local, sizes), mesh=mesh, in_specs=in_specs, out_specs=out_specs, check_vma=False
    )
```

```python
import functools

import jax
import jax.numpy as jnp
from jax import lax
from jax.experimental import pallas as pl
from jax.experimental.pallas import tpu as pltpu
from jax.sharding import PartitionSpec as P

label_weight = 0.2
loss_scale = 16.0
epsilon = 1e-05
MESH = pl.DeviceIdType.MESH


def kernel(
    sizes, th, tw, sh_in, gain_in, sw, labels_in, align_in, mask_in,
    rl_hbm, out_hbm,
    sh, gain, labels, align, mask, rl_out, lg_out, hg_out,
    tbuf, twv, wbuf, normed, acc, tin, bl, stats, inner_in, sibout, sibin, part, rin, lin, student_ref, packed, turned, pick_ref,
    tw_sem, own_sem, sw_sem, in_sem, out_sem,
    left_send, right_send, sib_send, z_recv, s_recv,
    x_send, x_recv, y_send, y_recv,
    acc_send, acc_recv,
    stat_send, stat_recv, inner_send, inner_recv,
    gs_send, gs_recv, ln_send, ln_recv,
):
    G, V, T, S, H, C, CW, RP, LAG, M, OWN = sizes
    NC = H * C
    VS = V * S
    M = M if T == 2 and V > 2 else NC
    g, v, t, s = (lax.axis_index(a) for a in ("groups", "vocab", "tokens", "section"))
    me = v * S + s
    rows = th.shape[0]
    R = rows // H
    fc = th.shape[1] // C
    F = sw.shape[0]
    half = F // 2
    wc = half // CW
    frames, DS = sh.shape
    N = tw.shape[1]
    w = DS // VS
    per = V // T
    rp = frames // RP

    def did(gg=None, vv=None, tt=None, ss=None):
        pick = lambda a, b: b if a is None else a
        return (pick(gg, g), pick(vv, v), pick(tt, t), pick(ss, s))

    def remote(src, dst, send, recv, where):
        return pltpu.make_async_remote_copy(
            src_ref=src, dst_ref=dst, send_sem=send, recv_sem=recv,
            device_id=where, device_id_type=MESH,
        )

    def vs_peer(k):
        other = lax.rem(me + k, VS)
        return did(vv=other // S, ss=lax.rem(other, S)), other

    def each(lo, hi, body):
        def run(i, carry):
            body(i)
            return carry
        lax.fori_loop(lo, hi, run, 0)

    barrier = pltpu.get_barrier_semaphore()

    def greet(where):
        pl.semaphore_signal(barrier, inc=1, device_id=where, device_id_type=MESH)

    loads = [
        pltpu.make_async_copy(source, target, in_sem.at[i])
        for i, (source, target) in enumerate(
            ((sh_in, sh), (gain_in, gain), (labels_in, labels), (align_in, align), (mask_in, mask))
        )
    ]
    for load in loads:
        load.start()
    def th_at(cc):
        h, c = cc // C, cc % C
        return th.at[h * R:(h + 1) * R, c * fc:(c + 1) * fc]

    for c in range(C):
        pltpu.make_async_copy(tw.at[c * fc:(c + 1) * fc], twv.at[c], tw_sem).start()
    for cc in range(NC):
        pltpu.make_async_copy(th_at(cc), tbuf.at[cc, me], own_sem).start()
    sw_copy = pltpu.make_async_copy(sw, wbuf.at[pl.ds(pl.multiple_of(t * F, F), F)], sw_sem)
    sw_copy.start()

    each(1, VS, lambda k: greet(vs_peer(k)[0]))
    each(1, T, lambda k: greet(did(tt=lax.rem(t + k, T))))
    greet(did(gg=1 - g))
    pl.semaphore_wait(barrier, VS - 1 + T - 1 + 1)

    def go_left(o, c, src):
        return remote(src, tbuf.at[c, o * S + s], left_send.at[o], z_recv.at[o, c], did(vv=v - 1))

    def go_right(o, c, src):
        return remote(src, tbuf.at[c, o * S + s], right_send.at[o], z_recv.at[o, c], did(vv=v + 1))

    def go_sib(o, c, src):
        return remote(src, tbuf.at[c, o * S + s], sib_send, s_recv.at[o, c], did(ss=1 - s))

    late_left = (v == 1) & (t == 0)
    late_right = (v == V - 2) & (t == T - 1)

    def send_own(lo, hi, to_left, to_right):
        for cc in range(lo, hi):
            @pl.when(to_left)
            def _():
                go_left(v, cc, th_at(cc)).start()

            @pl.when(to_right)
            def _():
                go_right(v, cc, th_at(cc)).start()

    send_own(0, M, v > 0, v < V - 1)
    send_own(M, NC, (v > 0) & jnp.logical_not(late_left), (v < V - 1) & jnp.logical_not(late_right))

    def w_at(tt, hh, cw):
        return wbuf.at[pl.ds(pl.multiple_of(tt * F + hh * half + cw * wc, wc), wc)]

    def go_x(k, cw):
        to = lax.rem(t + k, T)
        src = sw.at[pl.ds(pl.multiple_of(g * half + cw * wc, wc), wc)]
        return remote(src, w_at(t, g, cw), x_send.at[to], x_recv.at[k - 1, cw], did(tt=to))

    def go_y(tt, cw):
        return remote(w_at(tt, g, cw), w_at(tt, g, cw), y_send.at[tt], y_recv.at[tt], did(gg=1 - g))

    def x_wait(k, tt, cw):
        remote(w_at(tt, g, cw), w_at(tt, g, cw), x_send.at[tt], x_recv.at[k - 1, cw], did(tt=tt)).wait_recv()

    def w_half(tt, hh):
        return wbuf.at[pl.ds(pl.multiple_of(tt * F + hh * half, half), half)]

    def all_x(k):
        to = lax.rem(t + k, T)
        return remote(w_half(t, g), w_half(t, g), x_send.at[to], x_recv.at[0, 0], did(tt=to))

    def all_y(k, hh):
        tt = lax.rem(t + k, T)
        return remote(w_half(tt, hh), w_half(tt, hh), y_send.at[tt], y_recv.at[tt], did(gg=1 - g))

    nev = (T - 1) * CW
    each(0, nev, lambda j: go_x(j // CW + 1, lax.rem(j, CW)).start())
    for cc in range(NC):
        go_sib(v, cc, th_at(cc)).start()

    def pass_on(j):
        tt = lax.rem(t + T - 1 - j // CW, T)
        cw = lax.rem(j, CW)
        x_wait(j // CW + 1, tt, cw)
        go_y(tt, cw).start()

    for load in loads:
        load.wait()
    hid = sh[...].astype(jnp.float32)
    inverse = lax.rsqrt(jnp.mean(hid * hid, axis=1, keepdims=True) + epsilon)
    normed[...] = (hid * inverse * gain[...]).astype(jnp.bfloat16)

    def multiply(o, cc):
        x = tbuf[cc, pl.ds(o * S, S)].reshape(S * R, fc)
        acc[o, cc // C] += jnp.dot(x, twv[lax.rem(cc, C)], preferred_element_type=jnp.float32)

    def go_acc(o, h):
        p = lax.rem(o, per)
        return remote(acc.at[o, h], tin.at[t, p, h], acc_send, acc_recv.at[t], did(tt=o // per))

    def finished(o, cc):
        @pl.when((lax.rem(cc, C) == C - 1) & (o // per != t))
        def _():
            go_acc(o, cc // C).start()

    acc[...] = jnp.zeros_like(acc)

    pltpu.make_async_copy(tbuf.at[:, me], tbuf.at[:, me], own_sem).wait()
    pltpu.make_async_copy(twv, twv, tw_sem).wait()

    def own_chunk(c):
        other = tbuf.at[c, v * S + 1 - s]
        remote(other, other, sib_send, s_recv.at[v, c], did(ss=1 - s)).wait_recv()
        multiply(v, c)
        finished(v, c)

    spread_own = V > 2
    if not spread_own:
        each(0, NC, own_chunk)

    def take(o, c, onward, has_next):
        here = tbuf.at[c, o * S + s]
        remote(here, here, sib_send, z_recv.at[o, c], did(ss=1 - s)).wait_recv()

        @pl.when(has_next)
        def _():
            onward(o, c, here).start()

        go_sib(o, c, here).start()

    def use(o, c):
        other = tbuf.at[c, o * S + 1 - s]
        remote(other, other, sib_send, s_recv.at[o, c], did(ss=1 - s)).wait_recv()
        multiply(o, c)
        finished(o, c)

    lane_n = lax.broadcasted_iota(jnp.int32, (frames, N), 1)
    lane = lax.broadcasted_iota(jnp.int32, (frames, frames), 1)
    sub = lax.broadcasted_iota(jnp.int32, (frames, frames), 0)

    def to_columns(row):
        return jnp.transpose(jnp.broadcast_to(row, (frames, frames)))

    def is_label():
        label_col = to_columns(labels[...].astype(jnp.float32)).astype(jnp.int32)[:, 0:1]
        return (label_col - me * N) == lane_n

    steps = (V - 1) * NC
    stride = max(1, min((steps - 2) // nev, 2 * NC // CW))

    passed = (V - 2) * NC
    at_least = lambda i, a: jnp.minimum(jnp.maximum(i - a + 1, 0), 1)
    turn_left = (1 - at_least(v, 1)) * (1 - at_least(t, 1))
    turn_right = at_least(v, V - 1) * at_least(t, T - 1)

    def source(i, turn):
        j = i
        if M < NC:
            j = i + turn * ((NC - M) * at_least(i, M) - (passed + NC - M) * at_least(i, M + passed))
        return j // NC + 1, lax.rem(j, NC)

    def student_head():
        sw_copy.wait()
        each(1, T, lambda k: all_y(k, 1 - g).wait_recv())
        logits = jnp.dot(normed[...], wbuf[...], preferred_element_type=jnp.float32)
        label_logit = jnp.sum(jnp.where(is_label(), logits, 0.0), axis=1, keepdims=True)
        top = jnp.max(logits, axis=1, keepdims=True)
        total = jnp.sum(jnp.exp(logits - top), axis=1, keepdims=True)
        student_ref[...] = logits
        align_cols = to_columns(align[...].astype(jnp.float32)).astype(jnp.int32) - t * frames
        pick_ref[...] = (align_cols == lane).astype(jnp.bfloat16)
        packed[...] = jnp.where(lane == 3, top, jnp.where(lane == 4, total, jnp.where(lane == 5, label_logit, 0.0)))

    student_at = steps - 4 if nev * stride < steps - 4 else None

    def step(i):
        @pl.when(i < steps)
        def _():
            k, c = source(i, turn_left)

            @pl.when(v + k < V)
            def _():
                take(v + k, c, go_left, v > 0)

            k, c = source(i, turn_right)

            @pl.when(v - k >= 0)
            def _():
                take(v - k, c, go_right, v < V - 1)

        if M < NC:
            @pl.when(i == passed - 1)
            def _():
                send_own(M, NC, late_left, late_right)

        j = i // stride - 1

        @pl.when((lax.rem(i, stride) == 0) & (j >= 0) & (j < nev))
        def _():
            pass_on(j)

        if spread_own:
            @pl.when((lax.rem(i, OWN) == OWN - 1) & (i // OWN < NC))
            def _():
                own_chunk(i // OWN)

        if student_at is not None:
            @pl.when(i == student_at)
            def _():
                student_head()

        @pl.when(i > 0)
        def _():
            k, c = source(i - 1, turn_left)

            @pl.when(v + k < V)
            def _():
                use(v + k, c)

            k, c = source(i - 1, turn_right)

            @pl.when(v - k >= 0)
            def _():
                use(v - k, c)

    each(0, steps + 1, step)
    each(min(nev, steps // stride), nev, pass_on)

    if student_at is None:
        student_head()
    student = student_ref[...]
    onehot = is_label()
    def tin_wait(k):
        tt = lax.rem(t + k, T)
        remote(tin.at[tt], tin.at[tt], acc_send, acc_recv.at[tt], did(tt=tt)).wait_recv()

    each(1, T, tin_wait)
    for p in range(per):
        for h in range(H):
            total = acc[t * per + p, h]
            for k in range(1, T):
                total = total + tin[lax.rem(t + k, T), p, h]
            for ss in range(S):
                at = (p * S + ss) * rows + h * R
                bl[at:at + R, :] = total[ss * R:(ss + 1) * R]
    whole = bl[...]
    hi = whole.astype(jnp.bfloat16)
    rest = whole - hi.astype(jnp.float32)
    mid = rest.astype(jnp.bfloat16)
    low = (rest - mid.astype(jnp.float32)).astype(jnp.bfloat16)
    rows_of = lambda piece: jnp.dot(pick_ref[...], piece, preferred_element_type=jnp.float32)
    aligned = (rows_of(low) + rows_of(mid)) + rows_of(hi)
    top_t = jnp.max(aligned, axis=1, keepdims=True)
    exp_t = jnp.exp(aligned - top_t)
    sum_t = jnp.sum(exp_t, axis=1, keepdims=True)
    cross_t = jnp.sum(exp_t * (aligned - student), axis=1, keepdims=True)

    pack = packed[...]
    for i, column in enumerate((top_t, sum_t, cross_t)):
        pack = jnp.where(lane == i, column, pack)
    stats[me] = jnp.transpose(pack)[0:8, :]

    def go_stat(k):
        where, other = vs_peer(k)
        return remote(stats.at[me], stats.at[me], stat_send, stat_recv, where)

    def farthest_first(k):
        high = at_least(v, V // 2)
        return high * k + (1 - high) * (VS - k)

    each(1, VS, lambda k: go_stat(farthest_first(k)).start())

    def peers(buf, send, recv):
        return remote(buf.at[0:VS - 1], buf.at[0:VS - 1], send, recv, did(ss=1 - s))

    def turn_block(b):
        turned[b] = jnp.transpose(wbuf[pl.ds(pl.multiple_of(b * w, w), w), :])

    each(0, VS, turn_block)
    mask_float = mask[...].astype(jnp.float32)
    mask_count = jnp.sum(jnp.sum(mask_float, axis=1, keepdims=True), axis=0, keepdims=True)
    own_mask = mask[pl.ds(t, 1), :].astype(jnp.float32)
    row_weight = own_mask * (T * frames) / mask_count
    peers(stats, stat_send, stat_recv).wait_recv()
    st = stats[...]
    row = lambda i: st[:, i, :]
    all_t = jnp.max(row(0), axis=0, keepdims=True)
    all_s = jnp.max(row(3), axis=0, keepdims=True)
    scale_t = jnp.exp(row(0) - all_t)
    scale_s = jnp.exp(row(3) - all_s)
    add = lambda x: jnp.sum(x, axis=0, keepdims=True)
    total_t = add(row(1) * scale_t)
    lse_t = all_t + jnp.log(total_t)
    lse_s = all_s + jnp.log(add(row(4) * scale_s))
    diverge = add(row(2) * scale_t) / total_t - lse_t + lse_s
    cross_term = lse_s - add(row(5))
    rl_out[...] = row_weight * (diverge + label_weight * cross_term)

    unpacked = jnp.where(sub == 0, lse_t, jnp.where(sub == 1, lse_s, row_weight))
    columns = jnp.transpose(unpacked)
    teacher_prob = jnp.exp(aligned - columns[:, 0:1])
    student_prob = jnp.exp(student - columns[:, 1:2])
    grad = (
        loss_scale * columns[:, 2:3]
        * ((1.0 + label_weight) * student_prob - teacher_prob - label_weight * onehot.astype(jnp.float32))
    ).astype(jnp.bfloat16)
    lg_out[...] = grad
    stores = [
        pltpu.make_async_copy(source, target, out_sem.at[i])
        for i, (source, target) in enumerate((
            (rl_out, rl_hbm),
            (lg_out, out_hbm.at[:, 0:N]),
            (hg_out, out_hbm.at[:, N:]),
        ))
    ]
    stores[0].start()
    stores[1].start()

    def go_inner(k):
        where, other = vs_peer(k)
        return remote(inner_in.at[me], inner_in.at[me], inner_send, inner_recv, where)

    def term(block):
        return jnp.dot(lg_out[...], turned[block], preferred_element_type=jnp.float32)

    def piece(buf, b, p):
        return buf.at[b, pl.ds(pl.multiple_of(p * rp, rp), rp)]

    def go_gs(b, p):
        return remote(piece(sibout, b, p), piece(sibin, b, p), gs_send, gs_recv.at[b, p], did(ss=1 - s))

    def order(q):
        b = lax.rem(q, 2) * (q // 2) + (1 - lax.rem(q, 2)) * (V - 1 - q // 2)
        high = at_least(v, V // 2)
        return high * (V - 1 - b) + (1 - high) * b

    def first_sib(p):
        b = order(0)
        at = pl.ds(pl.multiple_of(p * rp, rp), rp)
        sibout[b, at] = jnp.dot(lg_out[at, :], turned[b * S + 1 - s], preferred_element_type=jnp.float32)
        go_gs(b, p).start()

    def for_sib(q):
        b = order(q)
        sibout[b] = term(b * S + 1 - s)
        each(0, RP, lambda p: go_gs(b, p).start())

    def for_own(q):
        b = order(q)
        part[b] = term(b * S + s)

    def go_line(buf, turn, b, p, onward):
        return remote(piece(part, b, p), piece(buf, b, p), ln_send, ln_recv.at[b + turn, p], did(vv=onward))

    def line(n, buf, turn, b_of, comes, onward):
        q, p = n // RP, lax.rem(n, RP)
        b = b_of(q)

        at = pl.ds(pl.multiple_of(p * rp, rp), rp)
        go_gs(b, p).wait_recv()
        part[b, at] += sibin[b, at]

        @pl.when(comes)
        def _():
            go_line(buf, turn, b, p, onward).wait_recv()
            part[b, at] += buf[b, at]

        go_line(buf, turn, b, p, onward).start()

    from_top, from_zero = (lambda q: V - 1 - q), (lambda q: q)

    def line_step(i):
        n = i - v * LAG

        @pl.when((n >= 0) & (n < (V - 1 - v) * RP))
        def _():
            line(n, rin, 1, from_top, v > 0, v + 1)

        m = i - (V - 1 - v) * LAG

        @pl.when((m >= 0) & (m < v * RP))
        def _():
            line(m, lin, 0, from_zero, v < V - 1, v - 1)

    each(0, RP, first_sib)
    for_own(0)
    for_sib(1)
    inner = jnp.sum(lg_out[...].astype(jnp.float32) * student_ref[...], axis=1, keepdims=True)
    inner_in[me] = jnp.transpose(jnp.broadcast_to(inner, (frames, frames)))[0:8, :]
    each(0, LAG, line_step)
    for_own(1)
    each(2, V, for_sib)
    each(2, V, for_own)
    each(1, VS, lambda k: go_inner(k).start())
    each(LAG, (V - 1) * max(RP, LAG), line_step)

    def sent(o):
        here = tbuf.at[:, o * S + s]

        @pl.when((o >= v) & (v > 0))
        def _():
            remote(here, here, left_send.at[o], z_recv.at[o, 0], did(vv=v - 1)).wait_send()

        @pl.when((o <= v) & (v < V - 1))
        def _():
            remote(here, here, right_send.at[o], z_recv.at[o, 0], did(vv=v + 1)).wait_send()


    each(0, V, sent)
    section = tbuf.at[:, 0:V]
    remote(section, section, sib_send, s_recv.at[0, 0], did(ss=1 - s)).wait_send()
    others = acc.at[0:V - per]
    remote(others, others, acc_send, acc_recv.at[t], did(ss=1 - s)).wait_send()

    def w_sent(k):
        all_x(k).wait_send()
        all_y(k, g).wait_send()

    each(1, T, w_sent)
    remote(sibout, sibout, gs_send, gs_recv.at[0, 0], did(ss=1 - s)).wait_send()
    peers(stats, stat_send, stat_recv).wait_send()
    peers(inner_in, inner_send, inner_recv).wait_send()
    peers(inner_in, inner_send, inner_recv).wait_recv()
    inner_total = jnp.sum(inner_in[...], axis=0)[0:1, :]
    inner_rows = to_columns(inner_total)[:, 0:1]

    each(0, RP, lambda p: go_gs(v, p).wait_recv())
    part[v] += sibin[v]

    def last(buf, turn, onward):
        each(0, RP, lambda p: go_line(buf, turn, v, p, onward).wait_recv())
        part[v] += buf[v]

    @pl.when(v > 0)
    def _():
        last(rin, 1, v - 1)

    @pl.when(v < V - 1)
    def _():
        last(lin, 0, v + 1)

    mine = pl.multiple_of(me * w, w)
    scaled = part[v] * gain[:, pl.ds(mine, w)]
    own_hidden = sh[:, pl.ds(mine, w)].astype(jnp.float32)
    hg_out[...] = (inverse * scaled - own_hidden * (inverse**2 * inner_rows / DS)).astype(jnp.bfloat16)

    stores[2].start()

    some = part.at[0:V - 1]
    remote(some, some, ln_send, ln_recv.at[0, 0], did(ss=1 - s)).wait_send()
    for store in stores:
        store.wait()


def spread(loss_in, both_in, loss_hbm, grad_hbm, hidden_hbm, loss, grad, hidden, sem):
    N = grad.shape[1]
    loads = [
        pltpu.make_async_copy(source, target, sem.at[i])
        for i, (source, target) in enumerate(
            ((both_in.at[:, 0:N], grad), (both_in.at[:, N:], hidden), (loss_in, loss))
        )
    ]
    stores = [
        pltpu.make_async_copy(source, target, sem.at[i])
        for i, (source, target) in enumerate(((grad, grad_hbm), (hidden, hidden_hbm), (loss, loss_hbm)))
    ]
    for load in loads:
        load.start()
    for load, store in zip(loads, stores):
        load.wait()
        store.start()
    for store in stores:
        store.wait()


def local(sizes, teacher_hidden, teacher_weight, student_hidden, student_gain, student_weight, labels, alignment, loss_mask):
    G, V, T, S, H, C, CW, RP, LAG, M, OWN = sizes
    VS = V * S
    NC = H * C
    rows, width = teacher_hidden.shape
    R = rows // H
    fc = width // C
    N = teacher_weight.shape[1]
    frames, DS = student_hidden.shape
    w = DS // VS
    per = V // T
    f32, bf16 = jnp.float32, jnp.bfloat16
    dma = pltpu.SemaphoreType.DMA
    hbm = pl.BlockSpec(memory_space=pl.ANY)
    row_loss, both = pl.pallas_call(
        functools.partial(kernel, sizes),
        out_shape=(jax.ShapeDtypeStruct((1, frames), f32), jax.ShapeDtypeStruct((frames, N + w), bf16)),
        in_specs=[hbm] * 8,
        out_specs=(hbm, hbm),
        scratch_shapes=[
            pltpu.VMEM((frames, DS), bf16),
            pltpu.VMEM((1, DS), f32),
            pltpu.VMEM((1, frames), jnp.int32),
            pltpu.VMEM((1, frames), jnp.int32),
            pltpu.VMEM((T, frames), jnp.int32),
            pltpu.VMEM((1, frames), f32),
            pltpu.VMEM((frames, N), bf16),
            pltpu.VMEM((frames, w), bf16),
            pltpu.VMEM((NC, VS, R, fc), bf16),
            pltpu.VMEM((C, fc, N), bf16),
            pltpu.VMEM((DS, N), bf16),
            pltpu.VMEM((frames, DS), bf16),
            pltpu.VMEM((V, H, S * R, N), f32),
            pltpu.VMEM((T, per, H, S * R, N), f32),
            pltpu.VMEM((frames, N), f32),
            pltpu.VMEM((VS, 8, frames), f32),
            pltpu.VMEM((VS, 8, frames), f32),
            pltpu.VMEM((V, frames, w), f32),
            pltpu.VMEM((V, frames, w), f32),
            pltpu.VMEM((V, frames, w), f32),
            pltpu.VMEM((V, frames, w), f32),
            pltpu.VMEM((V, frames, w), f32),
            pltpu.VMEM((frames, N), f32),
            pltpu.VMEM((frames, frames), f32),
            pltpu.VMEM((VS, N, w), bf16),
            pltpu.VMEM((frames, frames), bf16),
            dma, dma, dma, dma((5,)), dma((3,)),
            dma((V,)), dma((V,)), dma, dma((V, NC)), dma((V, NC)),
            dma((T,)), dma((T - 1, CW)), dma((T,)), dma((T,)),
            dma, dma((T,)),
            dma, dma, dma, dma,
            dma, dma((V, RP)), dma, dma((V + 1, RP)),
        ],
        compiler_params=pltpu.CompilerParams(
            collective_id=0, has_side_effects=True, vmem_limit_bytes=63 * 2**20
        ),
    )(
        teacher_hidden, teacher_weight, student_hidden, student_gain.reshape(1, DS), student_weight,
        labels.reshape(1, frames), alignment.reshape(1, frames), loss_mask.reshape(T, frames),
    )
    row_loss, logit_grad, hidden_grad = pl.pallas_call(
        spread,
        out_shape=(
            jax.ShapeDtypeStruct((1, frames), f32),
            jax.ShapeDtypeStruct((frames, N), bf16),
            jax.ShapeDtypeStruct((frames, w), bf16),
        ),
        in_specs=[hbm] * 2,
        out_specs=(hbm,) * 3,
        scratch_shapes=[pltpu.VMEM((1, frames), f32), pltpu.VMEM((frames, N), bf16), pltpu.VMEM((frames, w), bf16), dma((3,))],
    )(row_loss, both)
    return row_loss.reshape(frames), logit_grad, hidden_grad


def solution(mesh):
    sizes = tuple(mesh.shape[a] for a in ("groups", "vocab", "tokens", "section")) + (2, 4, 8, 4, 2, 4, 2)
    in_specs = (
        P(("groups", "vocab", "section"), "tokens"),
        P("tokens", ("vocab", "section")),
        P(("groups", "tokens"), None),
        P(),
        P("tokens", ("vocab", "section")),
        P(("groups", "tokens")),
        P(("groups", "tokens")),
        P("groups"),
    )
    out_specs = (
        P(("groups", "tokens")),
        P(("groups", "tokens"), ("vocab", "section")),
        P(("groups", "tokens"), ("vocab", "section")),
    )
    return jax.shard_map(
        functools.partial(local, sizes), mesh=mesh, in_specs=in_specs, out_specs=out_specs, check_vma=False
    )
```
